256 devices in a mesh: freq: 8 (over z), dom: 32 (over y, x, core).
Axes of the slice: x: 4, y: 4, z: 8, core: 2. Of those that a mesh axis runs over, the one named last changes fastest.
Arguments:
- angular: float32 [16], P('freq'), may hold values from 0.5 to 4
- stiffness: float32 [32, 36, 1024], P('dom'), as said below
- mass_matrix: float32 [32, 36, 1024], P('dom'), as said below
- conductivity: float32 [32, 1024], P('dom'), may hold values from 0.3 to 3
- element_edges: int32 [32, 6, 1024], P('dom'), may hold values from 0 to 1279
- live_slots: int32 [32, 1024], P('dom'), may hold values from 0 to 1, as said below
- adjoint_source: float32 [16, 2, 32, 1280], P('freq', None, 'dom'), may hold values from -6 to 6
- forward_field: float32 [16, 2, 32, 1280], P('freq', None, 'dom'), may hold values from -6 to 6
- neighbour_map: int32 [32, 256], P('dom'), may hold values from 0 to 255, each once within a row
Outputs:
- gradient: float32 [32, 1024], P('dom')
- updated_conductivity: float32 [32, 1024], P('dom')
The draws below stay inside these ranges and needn't reach their ends.
Inputs may be any that keep to these rules, and one draw needn't show every extreme that they name: `live_slots`: in each partition the live slots come first; at least half of the 1024 slots are live, and some partition has all slots live. `neighbour_map`: each row is a permutation of the rim slots; row 0 is not used. `stiffness`: each element matrix is symmetric with a strictly dominant positive diagonal. `mass_matrix`: each element matrix is symmetric with a strictly dominant positive diagonal.
All inputs are finite; a program needn't handle non-finite values.
Results may differ from the reference program's by a relative error of at most 0.0003.
Values sent between devices are 32-bit elements; how exact they have to be, the bound alone decides.
A program may use at most 64 MiB of HBM per device.

```python
import math
import jax
import jax.numpy as jnp
from jax import lax

ELEMS = 1024
EDGES = 1280
IFACE = 256
NPOL = 2
ITERS = 3
FREQS = 16
PARTS_SIZE = 32


def symmetric_blocks(key, diag_lo, diag_hi, spread):
    upper = jax.random.uniform(key, (PARTS_SIZE, 6, 6, ELEMS), jnp.float32, -spread, spread)
    upper = 0.5 * (upper + jnp.swapaxes(upper, 1, 2))
    diagonal = jax.random.uniform(jax.random.fold_in(key, 1), (PARTS_SIZE, 6, ELEMS), jnp.float32, diag_lo, diag_hi)
    identity = (jnp.arange(6)[:, None] == jnp.arange(6)[None, :]).astype(jnp.float32)[None, :, :, None]
    blocks = upper * (1.0 - identity) + identity * diagonal[:, :, None, :]
    return blocks.reshape(PARTS_SIZE, 36, ELEMS)


def draw_stiffness(key, part):
    return symmetric_blocks(jax.random.fold_in(key, 11), 1.8, 2.6, 0.35)


def draw_mass_matrix(key, part):
    return symmetric_blocks(jax.random.fold_in(key, 23), 1.0, 1.5, 0.2)


def draw_live_slots(key, part):
    counts = jax.random.randint(jax.random.fold_in(key, 31), (PARTS_SIZE,), ELEMS // 2, ELEMS + 1)
    chosen = jax.random.randint(jax.random.fold_in(key, 37), (), 0, PARTS_SIZE)
    counts = jnp.where(jnp.arange(PARTS_SIZE) == chosen, ELEMS, counts)
    return (jnp.arange(ELEMS)[None, :] < counts[:, None]).astype(jnp.int32)


def place_ends(values, key, least, largest):
    dims = values.shape
    spot = [jax.random.randint(jax.random.fold_in(key, axis), (), 0, dims[axis]) for axis in range(len(dims))]
    values = values.at[tuple(spot)].set(least)
    longest = dims.index(max(dims))
    spot[longest] = (spot[longest] + 1) % dims[longest]
    return values.at[tuple(spot)].set(largest)


def shard_levels(stream_key, extent, cuts, least, high):
    def one(axis_at, shards_of):
        steps = jax.random.uniform(jax.random.fold_in(jax.random.fold_in(stream_key, 6), axis_at), (shards_of,), jnp.float32, least / len(cuts), high / len(cuts))
        return jnp.repeat(jnp.exp(steps), extent[axis_at] // shards_of).reshape((-1,) + (1,) * (len(extent) - axis_at - 1))

    gain = one(*cuts[0])
    for cut in cuts[1:]:
        gain = gain * one(*cut)
    return gain


def scatter_about(key, shape, scale, bound, shards=(), kind=jnp.bfloat16):
    entries = jax.random.normal(key, shape, jnp.float32) * scale
    if len(shards) > 0:
        entries = shard_levels(key, shape, shards, -0.22, 0.18) * entries
    return jnp.clip(entries, min=-bound, max=bound).astype(kind)


def setup_inputs(seed: int = 0) -> dict:
    key_list = jax.random.split(jax.random.key(seed), 10)
    angular = jnp.clip(jnp.exp(math.log(4.0) - 2.0794415 * jax.random.uniform(key_list[0], (FREQS,), jnp.float32) ** shard_levels(key_list[0], (FREQS,), ((0, 8),), -0.2, 0.2)), 0.5, 4.0)
    stiffness = draw_stiffness(jax.random.fold_in(key_list[9], 71), 0)
    mass_matrix = draw_mass_matrix(jax.random.fold_in(key_list[9], 71), 0)
    conductivity = jnp.clip(jnp.exp(math.log(3.0) - 2.3025851 * jax.random.uniform(key_list[3], (PARTS_SIZE, ELEMS), jnp.float32) ** shard_levels(key_list[3], (PARTS_SIZE, ELEMS), ((0, 32),), -0.2, 0.2)), 0.3, 3.0)
    element_edges = place_ends(jax.random.randint(key_list[4], (PARTS_SIZE, 6, ELEMS), 0, EDGES), jax.random.fold_in(key_list[4], 1), 0, EDGES - 1).astype(jnp.int32)
    live_slots = draw_live_slots(jax.random.fold_in(key_list[9], 71), 0)
    adjoint_source = scatter_about(key_list[6], (FREQS, NPOL, PARTS_SIZE, EDGES), 1.0, 6.0, ((0, 8), (2, 32)), jnp.float32)
    forward_field = scatter_about(key_list[7], (FREQS, NPOL, PARTS_SIZE, EDGES), 1.0, 6.0, ((0, 8), (2, 32)), jnp.float32)
    neighbour_map = jax.vmap(lambda own: jax.random.permutation(own, IFACE))(jax.random.split(key_list[8], PARTS_SIZE)).reshape((PARTS_SIZE, IFACE)).astype(jnp.int32)
    return dict(angular=angular, stiffness=stiffness, mass_matrix=mass_matrix, conductivity=conductivity, element_edges=element_edges, live_slots=live_slots, adjoint_source=adjoint_source, forward_field=forward_field, neighbour_map=neighbour_map)


def element_blocks(angular, stiffness, mass_matrix, conductivity, live_slots):
    weights = live_slots.astype(jnp.float32)
    shifted = angular[:, None, None] * (conductivity * weights)[None, None, :]
    return stiffness[None] * weights[None, None, :] + shifted * mass_matrix[None]


def pick_edges(vector_in, edge_ids):
    groups = vector_in.shape[0]
    polars = vector_in.shape[1]
    return vector_in[:, :, edge_ids.reshape(-1)].reshape(groups, polars, 6, -1)


def element_apply(blocks, vector_in, edge_ids):
    picked = pick_edges(vector_in, edge_ids)
    stacked = []
    for i in range(6):
        running = blocks[:, None, 6 * i, :] * picked[:, :, 0, :]
        for j in range(1, 6):
            running = running + blocks[:, None, 6 * i + j, :] * picked[:, :, j, :]
        stacked.append(running)
    return jnp.stack(stacked, axis=2)


def scatter_edges(values, edge_ids, edge_count):
    flat_values = values.reshape(values.shape[0], values.shape[1], -1)
    flat_index = edge_ids.reshape(-1)

    def single(row_values):
        return jax.ops.segment_sum(row_values, flat_index, num_segments=edge_count)

    return jax.vmap(jax.vmap(single))(flat_values)


def element_gradient(angular, mass_matrix, live_slots, adjoint, forward_local, edge_ids):
    applied = element_apply(mass_matrix[None], forward_local, edge_ids)
    picked = pick_edges(adjoint, edge_ids)
    inner_terms = jnp.sum(picked * applied, axis=(1, 2))
    return -jnp.sum(angular[:, None] * inner_terms, axis=0) * live_slots.astype(jnp.float32)


def assemble(vectors, neighbour_map):
    lower_rim = vectors[..., :IFACE]
    upper_rim = vectors[..., EDGES - IFACE:]
    arranged = jax.vmap(lambda rim, order: jnp.zeros_like(rim).at[..., order].set(rim))(lower_rim, neighbour_map)
    previous = jnp.concatenate([jnp.zeros_like(upper_rim[:1]), upper_rim[:-1]], axis=0)
    from_below = jax.vmap(lambda rim, order: jnp.take(rim, order, axis=-1))(previous, neighbour_map)
    from_above = jnp.concatenate([arranged[1:], jnp.zeros_like(arranged[:1])], axis=0)
    middle = vectors[..., IFACE:EDGES - IFACE]
    return jnp.concatenate([lower_rim + from_below, middle, upper_rim + from_above], axis=-1)


def reference(angular, stiffness, mass_matrix, conductivity, element_edges, live_slots, adjoint_source, forward_field, neighbour_map):
    source_parts = jnp.transpose(adjoint_source, (2, 0, 1, 3))
    forward_parts = jnp.transpose(forward_field, (2, 0, 1, 3))
    positions = jnp.arange(EDGES)[None, :]
    part_ids = jnp.arange(PARTS_SIZE)[:, None]
    owned = jnp.where((positions < IFACE) & (part_ids > 0), 0.0, 1.0).astype(jnp.float32)

    def apply_all(vector_parts):
        def one_part(inputs):
            vector_in, stiff_part, mass_part, cond_part, edges_part, live_part = inputs
            blocks = element_blocks(angular, stiff_part, mass_part, cond_part, live_part)
            return scatter_edges(element_apply(blocks, vector_in, edges_part), edges_part, EDGES)

        local = lax.map(one_part, (vector_parts, stiffness, mass_matrix, conductivity, element_edges, live_slots))
        return assemble(local, neighbour_map)

    def inner(first, second):
        return jnp.sum(first * second * owned[:, None, None, :], axis=(0, 3))

    rhs = assemble(source_parts, neighbour_map)
    adjoint = jnp.zeros_like(rhs)
    residual = rhs
    direction = rhs
    norm_now = inner(residual, residual)
    for step in range(ITERS):
        image = apply_all(direction)
        alpha = (norm_now / inner(direction, image))[None, :, :, None]
        adjoint = adjoint + alpha * direction
        residual = residual - alpha * image
        norm_next = inner(residual, residual)
        direction = residual + (norm_next / norm_now)[None, :, :, None] * direction
        norm_now = norm_next

    def grad_part(inputs):
        adjoint_part, forward_part, mass_part, live_part, edges_part = inputs
        return element_gradient(angular, mass_part, live_part, adjoint_part, forward_part, edges_part)

    gradient = lax.map(grad_part, (adjoint, forward_parts, mass_matrix, live_slots, element_edges))
    updated = conductivity * jnp.exp(-0.5 * jnp.tanh(gradient))
    return gradient, updated
```

```python
import jax
import jax.numpy as jnp
from jax import lax
from jax.experimental import pallas as pl
from jax.experimental.pallas import tpu as pltpu
from jax.sharding import PartitionSpec as P

MESH = pl.DeviceIdType.MESH
F32 = jnp.float32
BF16 = jnp.bfloat16
DOM = 32
FREQ = 8
RIM = 256
EDGES = 1280
HALF = 512
CHUNKS = EDGES // 128
WIDE = EDGES // RIM
PARTS = 2


def rows_iota(shape):
    return lax.broadcasted_iota(jnp.int32, shape, 0)


def lanes_iota(shape):
    return lax.broadcasted_iota(jnp.int32, shape, 1)


def lane_pick(table, lane):
    return jnp.take_along_axis(table, lane, axis=1, mode="promise_in_bounds")


def two_halves(row):
    first = jnp.broadcast_to(row[:, :HALF], (8, HALF))
    second = jnp.broadcast_to(row[:, HALF:], (8, HALF))
    return jnp.where(rows_iota((8, HALF)) < 4, first, second)


def eight_rows(row):
    out = jnp.broadcast_to(row[:, :128], (8, 128))
    for r in range(1, 8):
        piece = jnp.broadcast_to(row[:, 128 * r : 128 * (r + 1)], (8, 128))
        out = jnp.where(rows_iota((8, 128)) == r, piece, out)
    return out


def field_rows(ref):
    out = jnp.broadcast_to(ref[0, 0], (8, EDGES))
    kind = rows_iota((8, EDGES)) % 4
    for v in range(1, 4):
        out = jnp.where(kind == v, jnp.broadcast_to(ref[v // 2, v % 2], (8, EDGES)), out)
    return out


def permuted(rim, order):
    out = []
    for q in range(2):
        index = order[:, 128 * q : 128 * (q + 1)]
        lane = index & 127
        low = lane_pick(rim[:, :128], lane)
        high = lane_pick(rim[:, 128:], lane)
        out.append(jnp.where(index < 128, low, high))
    return jnp.concatenate(out, axis=1)


def edge_dot(a, b, own=None):
    total = a[:, 256:384] * b[:, 256:384]
    for c in range(3, CHUNKS):
        total = total + a[:, 128 * c : 128 * (c + 1)] * b[:, 128 * c : 128 * (c + 1)]
    rim = a[:, :128] * b[:, :128] + a[:, 128:256] * b[:, 128:256]
    return total + (rim if own is None else own * rim)


def kernel(
    angular,
    stiffness_hbm,
    mass_hbm,
    conductivity_hbm,
    edges_hbm,
    live_hbm,
    source_hbm,
    forward_hbm,
    order_hbm,
    gradient_ref,
    updated_ref,
    stiffness,
    mass,
    conductivity,
    edges,
    live,
    source,
    forward,
    order,
    ids,
    masks,
    onehot,
    blocks,
    picked,
    weight,
    values,
    down_out,
    up_out,
    down_in,
    up_in,
    sums,
    terms,
    load_sem,
    down_send,
    down_recv,
    up_send,
    up_recv,
    sum_send,
    sum_recv,
    term_send,
    term_recv,
):
    me = lax.axis_index("dom")
    my_freq = lax.axis_index("freq")
    below = lax.rem(me + DOM - 1, DOM)
    above = lax.rem(me + 1, DOM)

    loads = [
        pltpu.make_async_copy(src, dst, load_sem.at[n])
        for n, (src, dst) in enumerate(
            [
                (source_hbm, source),
                (order_hbm, order),
                (edges_hbm.at[0], edges),
                (forward_hbm, forward),
                (conductivity_hbm, conductivity),
                (live_hbm, live),
                (stiffness_hbm.at[0], stiffness),
                (mass_hbm.at[0], mass),
            ]
        )
    ]
    for load in loads:
        load.start()

    barrier = pltpu.get_barrier_semaphore()
    for k in range(1, DOM):
        peer = lax.rem(me + k, DOM)
        pl.semaphore_signal(barrier, inc=1, device_id=(my_freq, peer), device_id_type=MESH)
    for k in range(1, FREQ):
        peer = lax.rem(my_freq + k, FREQ)
        pl.semaphore_signal(barrier, inc=1, device_id=(peer, me), device_id_type=MESH)

    loads[0].wait()
    loads[1].wait()
    order_rows = jnp.broadcast_to(order[...], (8, RIM))
    match = jnp.where(rows_iota((RIM, RIM)) == jnp.broadcast_to(order[...], (RIM, RIM)), 1.0, 0.0)
    inverse = lax.dot_general(
        lanes_iota((8, RIM)).astype(F32).astype(BF16),
        match.astype(BF16),
        (((1,), (1,)), ((), ())),
        preferred_element_type=F32,
    ).astype(jnp.int32)
    sources = field_rows(source)

    def send_rims(k, field):
        down_out[k] = permuted(field[:, :RIM], inverse)
        up_out[k] = field[:, EDGES - RIM :]
        copies = (
            pltpu.make_async_remote_copy(
                src_ref=down_out.at[k],
                dst_ref=down_in.at[k],
                send_sem=down_send.at[k],
                recv_sem=down_recv.at[k],
                device_id=(my_freq, below),
                device_id_type=MESH,
            ),
            pltpu.make_async_remote_copy(
                src_ref=up_out.at[k],
                dst_ref=up_in.at[k],
                send_sem=up_send.at[k],
                recv_sem=up_recv.at[k],
                device_id=(my_freq, above),
                device_id_type=MESH,
            ),
        )
        for copy in copies:
            copy.start()
        return copies

    def join_rims(k, copies, field):
        for copy in copies:
            copy.wait()
        zero = jnp.zeros((8, RIM), F32)
        from_below = jnp.where(me > 0, permuted(up_in[k], order_rows), zero)
        from_above = jnp.where(me < DOM - 1, down_in[k], zero)
        return jnp.concatenate(
            [
                field[:, :RIM] + from_below,
                field[:, RIM : EDGES - RIM],
                field[:, EDGES - RIM :] + from_above,
            ],
            axis=1,
        )

    pl.semaphore_wait(barrier, DOM - 1 + FREQ - 1)
    rim_copies = send_rims(0, sources)

    loads[2].wait()
    for i in range(6):
        row = edges[i : i + 1, :]
        ids[i] = two_halves(row)
        wide = ids[i] >> 8
        for c in range(WIDE):
            hit = jnp.where(wide == c, 1.0, 0.0)
            masks[c, :, HALF * i : HALF * (i + 1)] = jnp.concatenate([hit] * PARTS, axis=0).astype(BF16)
        for h in range(2):
            low = jnp.broadcast_to(row[:, HALF * h : HALF * (h + 1)] & (RIM - 1), (RIM, HALF))
            hit = jnp.where(rows_iota((RIM, HALF)) == low, 1.0, 0.0)
            onehot[RIM * h : RIM * (h + 1), HALF * i : HALF * (i + 1)] = hit.astype(BF16)

    def pick(field):
        def one(i, carry):
            for q in range(4):
                index = ids[i, :, 128 * q : 128 * (q + 1)]
                lane = index & 127
                found = [lane_pick(field[:, 128 * c : 128 * (c + 1)], lane) for c in range(CHUNKS)]
                bit = 7
                while len(found) > 1:
                    odd = (index & (1 << bit)) != 0
                    merged = [
                        jnp.where(odd, found[n + 1], found[n]) for n in range(0, len(found) - 1, 2)
                    ]
                    if len(found) % 2:
                        merged.append(found[-1])
                    found = merged
                    bit += 1
                picked[i, :, 128 * q : 128 * (q + 1)] = found[0]
            return carry

        for i in range(6):
            one(i, 0)

    loads[3].wait()
    pick(field_rows(forward))
    loads[4].wait()
    loads[5].wait()
    alive = two_halves(live[...]).astype(F32)
    cond_rows = two_halves(conductivity[...])
    freq_of = rows_iota((8, HALF)) % 4 < 2
    omega = jnp.where(freq_of, angular[0], angular[1])
    shift = omega * (cond_rows * alive)
    sign = -(omega * alive)
    cond_eight = eight_rows(conductivity[...])
    loads[6].wait()
    loads[7].wait()
    for i in range(6):
        running = None
        for j in range(6):
            n = 6 * i + j
            mass_rows = two_halves(mass[n : n + 1, :])
            blocks[n] = two_halves(stiffness[n : n + 1, :]) * alive + shift * mass_rows
            product = mass_rows * picked[j]
            running = product if running is None else running + product
        weight[i] = sign * running

    def apply(field):
        pick(field)
        term = weight[0] * picked[0]
        for i in range(1, 6):
            term = term + weight[i] * picked[i]
        for i in range(6):
            running = blocks[6 * i] * picked[0]
            for j in range(1, 6):
                running = running + blocks[6 * i + j] * picked[j]
            pieces = []
            rest = running
            for _ in range(PARTS - 1):
                head = rest.astype(BF16).astype(F32)
                pieces.append(head)
                rest = rest - head
            pieces.append(rest)
            stacked = jnp.concatenate(pieces, axis=0).astype(BF16)
            for c in range(WIDE):
                values[8 * PARTS * c : 8 * PARTS * (c + 1), HALF * i : HALF * (i + 1)] = (
                    stacked * masks[c, :, HALF * i : HALF * (i + 1)]
                )
        out = lax.dot_general(
            values[...], onehot[...], (((1,), (1,)), ((), ())), preferred_element_type=F32
        )
        pieces = []
        for c in range(WIDE):
            halves = out[8 * PARTS * c : 8 * PARTS * c + 8]
            for s in range(1, PARTS):
                halves = halves + out[8 * PARTS * c + 8 * s : 8 * PARTS * c + 8 * s + 8]
            mixed = jnp.where(rows_iota((8, RIM)) < 4, halves[:, :RIM], halves[:, RIM:])
            pieces.append(mixed + pltpu.roll(mixed, 4, 0))
        return jnp.concatenate(pieces, axis=1), term

    lane = lanes_iota((8, 128))
    sub = rows_iota((8, 128))

    def send_sums(k, quantities):
        row = jnp.zeros((8, 128), F32)
        for n, quantity in enumerate(quantities):
            column = jnp.sum(quantity, axis=1, keepdims=True)
            row = row + jnp.where((lane == 4 * n + sub) & (sub < 4), column, 0.0)
        sums[k, me] = jnp.sum(row, axis=0, keepdims=True)
        copies = []
        for n in range(1, DOM):
            peer = lax.rem(me + n, DOM)
            copy = pltpu.make_async_remote_copy(
                src_ref=sums.at[k, me],
                dst_ref=sums.at[k, me],
                send_sem=sum_send.at[k],
                recv_sem=sum_recv.at[k],
                device_id=(my_freq, peer),
                device_id_type=MESH,
            )
            copy.start()
            copies.append(copy)

    def take_sums(k, count):
        rest = sums.at[k, pl.ds(0, DOM - 1)]
        pltpu.make_async_copy(rest, rest, sum_recv.at[k]).wait()
        total = jnp.broadcast_to(jnp.sum(sums[k], axis=0), (8, 128))
        return [
            jnp.sum(jnp.where(lane == 4 * n + sub % 4, total, 0.0), axis=1, keepdims=True)
            for n in range(count)
        ]

    own = jnp.where(me > 0, 0.0, 1.0).astype(F32)

    base = join_rims(0, rim_copies, sources)
    image0, term0 = apply(base)
    send_sums(0, [edge_dot(base, base, own), edge_dot(base, image0)])
    rim_copies = send_rims(1, image0)
    first = join_rims(1, rim_copies, image0)
    image1, term1 = apply(first)
    rim_copies = send_rims(2, image1)

    norm0, curve0 = take_sums(0, 2)
    alpha0 = norm0 / curve0
    residual1 = base - alpha0 * first
    local1 = image0 - alpha0 * image1
    send_sums(
        1,
        [
            edge_dot(residual1, residual1, own),
            edge_dot(residual1, local1),
            edge_dot(residual1, image0) + edge_dot(base, local1),
        ],
    )
    second = join_rims(2, rim_copies, image1)
    image2, term2 = apply(second)

    norm1, self1, cross1 = take_sums(1, 3)
    beta0 = norm1 / norm0
    curve1 = self1 + beta0 * cross1 + (beta0 * beta0) * curve0
    alpha1 = norm1 / curve1
    direction1 = residual1 + beta0 * base
    along1 = local1 + beta0 * image0
    residual2 = residual1 - alpha1 * ((first - alpha0 * second) + beta0 * first)
    local2 = local1 - alpha1 * ((image1 - alpha0 * image2) + beta0 * image1)
    send_sums(
        2,
        [
            edge_dot(residual2, residual2, own),
            edge_dot(residual2, local2),
            edge_dot(residual2, along1) + edge_dot(direction1, local2),
        ],
    )
    near1 = term0 - alpha0 * term1
    toward1 = near1 + beta0 * term0
    near2 = near1 - alpha1 * ((term1 - alpha0 * term2) + beta0 * term1)
    so_far = alpha0 * term0 + alpha1 * toward1

    norm2, self2, cross2 = take_sums(2, 3)
    beta1 = norm2 / norm1
    curve2 = self2 + beta1 * cross2 + (beta1 * beta1) * curve1
    alpha2 = norm2 / curve2
    total = so_far + alpha2 * (near2 + beta1 * toward1)

    total = total + pltpu.roll(total, 1, 0)
    total = total + pltpu.roll(total, 2, 0)
    packed = jnp.zeros((8, 128), F32)
    for h in range(2):
        for q in range(4):
            piece = jnp.broadcast_to(total[4 * h + 3 : 4 * h + 4, 128 * q : 128 * (q + 1)], (8, 128))
            packed = jnp.where(sub == 4 * h + q, piece, packed)
    terms[my_freq] = packed
    for n in range(1, FREQ):
        peer = lax.rem(my_freq + n, FREQ)
        pltpu.make_async_remote_copy(
            src_ref=terms.at[my_freq],
            dst_ref=terms.at[my_freq],
            send_sem=term_send,
            recv_sem=term_recv,
            device_id=(peer, me),
            device_id_type=MESH,
        ).start()
    rest = terms.at[pl.ds(0, FREQ - 1)]
    pltpu.make_async_copy(rest, rest, term_recv).wait()
    gradient = terms[0]
    for n in range(1, FREQ):
        gradient = gradient + terms[n]
    updated = cond_eight * jnp.exp(-0.5 * jnp.tanh(gradient))
    for r in range(8):
        gradient_ref[:, 128 * r : 128 * (r + 1)] = gradient[r : r + 1]
        updated_ref[:, 128 * r : 128 * (r + 1)] = updated[r : r + 1]

    pltpu.make_async_copy(rest, rest, term_send).wait()
    for k in range(3):
        sent = sums.at[k, pl.ds(0, DOM - 1)]
        pltpu.make_async_copy(sent, sent, sum_send.at[k]).wait()


def local(*args):
    hbm = pl.BlockSpec(memory_space=pltpu.MemorySpace.HBM)
    dma = pltpu.SemaphoreType.DMA
    outs = [jax.ShapeDtypeStruct((1, 1024), F32)] * 2
    return pl.pallas_call(
        kernel,
        out_shape=outs,
        in_specs=[pl.BlockSpec(memory_space=pltpu.MemorySpace.SMEM)] + [hbm] * 8,
        out_specs=[pl.BlockSpec(memory_space=pltpu.MemorySpace.VMEM)] * 2,
        scratch_shapes=[
            pltpu.VMEM((36, 1024), F32),
            pltpu.VMEM((36, 1024), F32),
            pltpu.VMEM((1, 1024), F32),
            pltpu.VMEM((6, 1024), jnp.int32),
            pltpu.VMEM((1, 1024), jnp.int32),
            pltpu.VMEM((2, 2, 1, EDGES), F32),
            pltpu.VMEM((2, 2, 1, EDGES), F32),
            pltpu.VMEM((1, RIM), jnp.int32),
            pltpu.VMEM((6, 8, HALF), jnp.int32),
            pltpu.VMEM((WIDE, 8 * PARTS, 6 * HALF), BF16),
            pltpu.VMEM((2 * RIM, 6 * HALF), BF16),
            pltpu.VMEM((36, 8, HALF), F32),
            pltpu.VMEM((6, 8, HALF), F32),
            pltpu.VMEM((6, 8, HALF), F32),
            pltpu.VMEM((8 * PARTS * WIDE, 6 * HALF), BF16),
            pltpu.VMEM((3, 8, RIM), F32),
            pltpu.VMEM((3, 8, RIM), F32),
            pltpu.VMEM((3, 8, RIM), F32),
            pltpu.VMEM((3, 8, RIM), F32),
            pltpu.VMEM((3, DOM, 1, 128), F32),
            pltpu.VMEM((FREQ, 8, 128), F32),
            dma((8,)),
            dma((3,)),
            dma((3,)),
            dma((3,)),
            dma((3,)),
            dma((3,)),
            dma((3,)),
            dma,
            dma,
        ],
        compiler_params=pltpu.CompilerParams(collective_id=0, has_side_effects=True),
    )(*args)


def solution(mesh):
    return jax.shard_map(
        lambda *args: tuple(local(*args)),
        mesh=mesh,
        in_specs=(
            P("freq"),
            P("dom", None, None),
            P("dom", None, None),
            P("dom", None),
            P("dom", None, None),
            P("dom", None),
            P("freq", None, "dom", None),
            P("freq", None, "dom", None),
            P("dom", None),
        ),
        out_specs=(P("dom", None), P("dom", None)),
        check_vma=False,
    )
```

```python
import jax
import jax.numpy as jnp
from jax import lax
from jax.experimental import pallas as pl
from jax.experimental.pallas import tpu as pltpu
from jax.sharding import PartitionSpec as P

MESH = pl.DeviceIdType.MESH
F32 = jnp.float32
BF16 = jnp.bfloat16
DOM = 32
FREQ = 8
RIM = 256
EDGES = 1280
CHUNKS = EDGES // 128
GROUPS = 4
PARTS = 2
STACK = 8 * PARTS


def rows_iota(shape):
    return lax.broadcasted_iota(jnp.int32, shape, 0)


def lanes_iota(shape):
    return lax.broadcasted_iota(jnp.int32, shape, 1)


def lane_pick(table, lane):
    return jnp.take_along_axis(table, lane, axis=1, mode="promise_in_bounds")


def spread(row):
    return jnp.broadcast_to(row, (8, 128))


def chunk(field, c):
    return field[:, 128 * c : 128 * (c + 1)]


def field_rows(ref):
    out = jnp.broadcast_to(ref[0, 0], (8, EDGES))
    kind = rows_iota((8, EDGES)) % 4
    for v in range(1, 4):
        out = jnp.where(kind == v, jnp.broadcast_to(ref[v // 2, v % 2], (8, EDGES)), out)
    return out


def permuted(rim, order):
    out = []
    for q in range(2):
        index = chunk(order, q)
        lane = index & 127
        low = lane_pick(rim[:, :128], lane)
        high = lane_pick(rim[:, 128:], lane)
        out.append(jnp.where(index < 128, low, high))
    return jnp.concatenate(out, axis=1)


def pick(field, index):
    lane = index & 127
    found = [lane_pick(chunk(field, c), lane) for c in range(CHUNKS)]
    bit = 7
    while len(found) > 1:
        odd = (index & (1 << bit)) != 0
        merged = [jnp.where(odd, found[n + 1], found[n]) for n in range(0, len(found) - 1, 2)]
        if len(found) % 2:
            merged.append(found[-1])
        found = merged
        bit += 1
    return found[0]


def edge_dot(a, b, own=None):
    total = chunk(a, 2) * chunk(b, 2)
    for c in range(3, CHUNKS):
        total = total + chunk(a, c) * chunk(b, c)
    rim = chunk(a, 0) * chunk(b, 0) + chunk(a, 1) * chunk(b, 1)
    return total + (rim if own is None else own * rim)


def kernel(
    angular_hbm,
    stiffness_hbm,
    mass_hbm,
    conductivity_hbm,
    edges_hbm,
    live_hbm,
    source_hbm,
    forward_hbm,
    order_hbm,
    total_ref,
    angular,
    stiffness,
    mass,
    conductivity,
    edges,
    live,
    source,
    forward,
    order,
    ids,
    masks,
    onehot,
    blocks,
    weight,
    values,
    down_out,
    up_out,
    down_in,
    up_in,
    sums,
    terms,
    load_sem,
    down_send,
    down_recv,
    up_send,
    up_recv,
    sum_send,
    sum_recv,
    term_send,
    term_recv,
):
    me = lax.axis_index("dom")
    my_freq = lax.axis_index("freq")
    below = lax.rem(me + DOM - 1, DOM)
    above = lax.rem(me + 1, DOM)

    loads = [
        pltpu.make_async_copy(src, dst, load_sem.at[n])
        for n, (src, dst) in enumerate(
            [
                (source_hbm, source),
                (order_hbm, order),
                (edges_hbm, edges),
                (forward_hbm, forward),
                (stiffness_hbm, stiffness),
                (mass_hbm, mass),
                (conductivity_hbm, conductivity),
                (live_hbm, live),
                (angular_hbm, angular),
            ]
        )
    ]
    for load in loads:
        load.start()

    barrier = pltpu.get_barrier_semaphore()
    for k in range(1, DOM):
        peer = lax.rem(me + k, DOM)
        pl.semaphore_signal(barrier, inc=1, device_id=(my_freq, peer), device_id_type=MESH)
    for k in range(1, FREQ):
        peer = lax.rem(my_freq + k, FREQ)
        pl.semaphore_signal(barrier, inc=1, device_id=(peer, me), device_id_type=MESH)

    lane = lanes_iota((8, 128))
    sub = rows_iota((8, 128))
    upper = sub < 4

    def halves(ref, n, q):
        first = ref[n, :, pl.ds(pl.multiple_of(128 * q, 128), 128)]
        second = ref[n, :, pl.ds(pl.multiple_of(512 + 128 * q, 128), 128)]
        return jnp.where(upper, spread(first), spread(second))

    loads[0].wait()
    loads[1].wait()
    order_rows = jnp.broadcast_to(order[...], (8, RIM))
    match = jnp.where(rows_iota((RIM, RIM)) == jnp.broadcast_to(order[...], (RIM, RIM)), 1.0, 0.0)
    inverse = lax.dot_general(
        lanes_iota((8, RIM)).astype(F32).astype(BF16),
        match.astype(BF16),
        (((1,), (1,)), ((), ())),
        preferred_element_type=F32,
    ).astype(jnp.int32)
    sources = field_rows(source)

    loads[2].wait()

    def tables(q, carry):
        for i in range(6):
            index = halves(edges, i, q)
            ids[q, i] = index
            wide = index >> 7
            for c in range(CHUNKS):
                hit = jnp.where(wide == c, 1.0, 0.0)
                masks[q, c, :, 128 * i : 128 * (i + 1)] = jnp.concatenate([hit] * PARTS, axis=0).astype(BF16)
        for h in range(2):
            at = pl.ds(pl.multiple_of(512 * h + 128 * q, 128), 128)
            stacked = spread(edges[0, :, at])
            for i in range(1, 6):
                stacked = jnp.where(sub == i, spread(edges[i, :, at]), stacked)
            columns = jnp.transpose(stacked & 127)
            for i in range(6):
                hit = jnp.broadcast_to(columns[:, i : i + 1], (128, 128)) == lanes_iota((128, 128))
                onehot[q, 128 * i : 128 * (i + 1), 128 * h : 128 * (h + 1)] = jnp.where(hit, 1.0, 0.0).astype(BF16)
        return carry

    lax.fori_loop(0, GROUPS, tables, 0)

    def send_rims(k, field):
        down_out[k] = permuted(field[:, :RIM], inverse)
        up_out[k] = field[:, EDGES - RIM :]
        copies = (
            pltpu.make_async_remote_copy(
                src_ref=down_out.at[k],
                dst_ref=down_in.at[k],
                send_sem=down_send.at[k],
                recv_sem=down_recv.at[k],
                device_id=(my_freq, below),
                device_id_type=MESH,
            ),
            pltpu.make_async_remote_copy(
                src_ref=up_out.at[k],
                dst_ref=up_in.at[k],
                send_sem=up_send.at[k],
                recv_sem=up_recv.at[k],
                device_id=(my_freq, above),
                device_id_type=MESH,
            ),
        )
        for copy in copies:
            copy.start()
        return copies

    def join_rims(k, copies, field):
        for copy in copies:
            copy.wait_recv()
        zero = jnp.zeros((8, RIM), F32)
        from_below = jnp.where(me > 0, permuted(up_in[k], order_rows), zero)
        from_above = jnp.where(me < DOM - 1, down_in[k], zero)
        return jnp.concatenate(
            [
                field[:, :RIM] + from_below,
                field[:, RIM : EDGES - RIM],
                field[:, EDGES - RIM :] + from_above,
            ],
            axis=1,
        )

    pl.semaphore_wait(barrier, DOM - 1 + FREQ - 1)
    rims0 = send_rims(0, sources)

    for n in range(3, 9):
        loads[n].wait()
    omega = jnp.where(sub % 4 < 2, angular[0], angular[1])
    forwards = field_rows(forward)

    def elements(q, carry):
        alive = halves(live, 0, q).astype(F32)
        shift = omega * (halves(conductivity, 0, q) * alive)
        picked = [pick(forwards, ids[q, j]) for j in range(6)]
        for i in range(6):
            running = None
            for j in range(6):
                n = 6 * i + j
                mass_rows = halves(mass, n, q)
                blocks[q, n] = halves(stiffness, n, q) * alive + shift * mass_rows
                product = mass_rows * picked[j]
                running = product if running is None else running + product
            weight[q, i] = omega * running
        return carry

    lax.fori_loop(0, GROUPS, elements, 0)

    def apply(field):
        out = None
        terms_of = []
        for q in range(GROUPS):
            picked = [pick(field, ids[q, i]) for i in range(6)]
            term = weight[q, 0] * picked[0]
            for i in range(1, 6):
                term = term + weight[q, i] * picked[i]
            terms_of.append(term)
            for i in range(6):
                running = blocks[q, 6 * i] * picked[0]
                for j in range(1, 6):
                    running = running + blocks[q, 6 * i + j] * picked[j]
                pieces = []
                rest = running
                for _ in range(PARTS - 1):
                    head = rest.astype(BF16).astype(F32)
                    pieces.append(head)
                    rest = rest - head
                pieces.append(rest)
                stacked = jnp.concatenate(pieces, axis=0).astype(BF16)
                for c in range(CHUNKS):
                    values[q, STACK * c : STACK * (c + 1), 128 * i : 128 * (i + 1)] = (
                        stacked * masks[q, c, :, 128 * i : 128 * (i + 1)]
                    )
            product = lax.dot_general(
                values[q], onehot[q], (((1,), (0,)), ((), ())), preferred_element_type=F32
            )
            out = product if out is None else out + product
        pieces = []
        for c in range(CHUNKS):
            both = out[STACK * c : STACK * c + 8]
            for s in range(1, PARTS):
                both = both + out[STACK * c + 8 * s : STACK * c + 8 * s + 8]
            mixed = jnp.where(upper, both[:, :128], both[:, 128:])
            pieces.append(mixed + pltpu.roll(mixed, 4, 0))
        return jnp.concatenate(pieces, axis=1), jnp.concatenate(terms_of, axis=1)

    def send_sums(k, quantities):
        row = jnp.zeros((8, 128), F32)
        for n, quantity in enumerate(quantities):
            column = jnp.sum(quantity, axis=1, keepdims=True)
            row = row + jnp.where((lane == 4 * n + sub) & upper, column, 0.0)
        sums[k, me] = jnp.sum(row, axis=0, keepdims=True)
        for n in range(1, DOM):
            peer = lax.rem(me + n, DOM)
            pltpu.make_async_remote_copy(
                src_ref=sums.at[k, me],
                dst_ref=sums.at[k, me],
                send_sem=sum_send.at[k],
                recv_sem=sum_recv.at[k],
                device_id=(my_freq, peer),
                device_id_type=MESH,
            ).start()

    def take_sums(k, count):
        rest = sums.at[k, pl.ds(0, DOM - 1)]
        pltpu.make_async_copy(rest, rest, sum_recv.at[k]).wait()
        total = spread(jnp.sum(sums[k], axis=0))
        return [
            jnp.sum(jnp.where(lane == 4 * n + sub % 4, total, 0.0), axis=1, keepdims=True)
            for n in range(count)
        ]

    own = jnp.where(me > 0, 0.0, 1.0).astype(F32)

    base = join_rims(0, rims0, sources)
    image0, term0 = apply(base)
    rims1 = send_rims(1, image0)
    send_sums(0, [edge_dot(base, base, own), edge_dot(base, image0)])
    first = join_rims(1, rims1, image0)
    image1, term1 = apply(first)
    rims2 = send_rims(2, image1)

    norm0, curve0 = take_sums(0, 2)
    alpha0 = norm0 / curve0
    residual1 = base - alpha0 * first
    local1 = image0 - alpha0 * image1
    send_sums(
        1,
        [
            edge_dot(residual1, residual1, own),
            edge_dot(residual1, local1),
            edge_dot(residual1, image0) + edge_dot(base, local1),
        ],
    )
    second = join_rims(2, rims2, image1)
    image2, term2 = apply(second)

    norm1, self1, cross1 = take_sums(1, 3)
    beta0 = norm1 / norm0
    curve1 = self1 + beta0 * cross1 + (beta0 * beta0) * curve0
    alpha1 = norm1 / curve1
    direction1 = residual1 + beta0 * base
    along1 = local1 + beta0 * image0
    residual2 = residual1 - alpha1 * ((first - alpha0 * second) + beta0 * first)
    local2 = local1 - alpha1 * ((image1 - alpha0 * image2) + beta0 * image1)
    send_sums(
        2,
        [
            edge_dot(residual2, residual2, own),
            edge_dot(residual2, local2),
            edge_dot(residual2, along1) + edge_dot(direction1, local2),
        ],
    )
    near1 = term0 - alpha0 * term1
    toward1 = near1 + beta0 * term0
    near2 = near1 - alpha1 * ((term1 - alpha0 * term2) + beta0 * term1)
    so_far = alpha0 * term0 + alpha1 * toward1

    norm2, self2, cross2 = take_sums(2, 3)
    beta1 = norm2 / norm1
    curve2 = self2 + beta1 * cross2 + (beta1 * beta1) * curve1
    alpha2 = norm2 / curve2
    total = so_far + alpha2 * (near2 + beta1 * toward1)

    total = total + pltpu.roll(total, 1, 0)
    total = total + pltpu.roll(total, 2, 0)
    packed = jnp.zeros((8, 128), F32)
    for h in range(2):
        for q in range(GROUPS):
            piece = spread(total[4 * h + 3 : 4 * h + 4, 128 * q : 128 * (q + 1)])
            packed = jnp.where(sub == 4 * h + q, piece, packed)
    terms[my_freq] = packed
    for n in range(1, FREQ):
        peer = lax.rem(my_freq + n, FREQ)
        pltpu.make_async_remote_copy(
            src_ref=terms.at[my_freq],
            dst_ref=terms.at[my_freq],
            send_sem=term_send,
            recv_sem=term_recv,
            device_id=(peer, me),
            device_id_type=MESH,
        ).start()
    for copy in rims0 + rims1 + rims2:
        copy.wait_send()
    for k in range(3):
        sent = sums.at[k, pl.ds(0, DOM - 1)]
        pltpu.make_async_copy(sent, sent, sum_send.at[k]).wait()
    rest = terms.at[pl.ds(0, FREQ - 1)]
    pltpu.make_async_copy(rest, rest, term_recv).wait()
    added = terms[0]
    for n in range(1, FREQ):
        added = added + terms[n]
    for r in range(8):
        total_ref[:, 128 * r : 128 * (r + 1)] = added[r : r + 1]
    pltpu.make_async_copy(rest, rest, term_send).wait()


def local(
    angular,
    stiffness,
    mass_matrix,
    conductivity,
    element_edges,
    live_slots,
    adjoint_source,
    forward_field,
    neighbour_map,
):
    hbm = pl.BlockSpec(memory_space=pltpu.MemorySpace.HBM)
    dma = pltpu.SemaphoreType.DMA
    total = pl.pallas_call(
        kernel,
        out_shape=jax.ShapeDtypeStruct((1, 1024), F32),
        in_specs=[hbm] * 9,
        out_specs=pl.BlockSpec(memory_space=pltpu.MemorySpace.VMEM),
        scratch_shapes=[
            pltpu.SMEM((2,), F32),
            pltpu.VMEM((36, 1, 1024), F32),
            pltpu.VMEM((36, 1, 1024), F32),
            pltpu.VMEM((1, 1, 1024), F32),
            pltpu.VMEM((6, 1, 1024), jnp.int32),
            pltpu.VMEM((1, 1, 1024), jnp.int32),
            pltpu.VMEM((2, 2, 1, EDGES), F32),
            pltpu.VMEM((2, 2, 1, EDGES), F32),
            pltpu.VMEM((1, RIM), jnp.int32),
            pltpu.VMEM((GROUPS, 6, 8, 128), jnp.int32),
            pltpu.VMEM((GROUPS, CHUNKS, STACK, 768), BF16),
            pltpu.VMEM((GROUPS, 768, 256), BF16),
            pltpu.VMEM((GROUPS, 36, 8, 128), F32),
            pltpu.VMEM((GROUPS, 6, 8, 128), F32),
            pltpu.VMEM((GROUPS, STACK * CHUNKS, 768), BF16),
            pltpu.VMEM((3, 8, RIM), F32),
            pltpu.VMEM((3, 8, RIM), F32),
            pltpu.VMEM((3, 8, RIM), F32),
            pltpu.VMEM((3, 8, RIM), F32),
            pltpu.VMEM((3, DOM, 1, 128), F32),
            pltpu.VMEM((FREQ, 8, 128), F32),
            dma((9,)),
            dma((3,)),
            dma((3,)),
            dma((3,)),
            dma((3,)),
            dma((3,)),
            dma((3,)),
            dma,
            dma,
        ],
        compiler_params=pltpu.CompilerParams(collective_id=0, has_side_effects=True),
    )(
        angular,
        jnp.transpose(stiffness, (1, 0, 2)),
        jnp.transpose(mass_matrix, (1, 0, 2)),
        conductivity[None],
        jnp.transpose(element_edges, (1, 0, 2)),
        live_slots[None],
        adjoint_source,
        forward_field,
        neighbour_map,
    )
    gradient = -total * live_slots.astype(F32)
    updated = conductivity * jnp.exp(-0.5 * jnp.tanh(gradient))
    return gradient, updated


def solution(mesh):
    return jax.shard_map(
        local,
        mesh=mesh,
        in_specs=(
            P("freq"),
            P("dom", None, None),
            P("dom", None, None),
            P("dom", None),
            P("dom", None, None),
            P("dom", None),
            P("freq", None, "dom", None),
            P("freq", None, "dom", None),
            P("dom", None),
        ),
        out_specs=(P("dom", None), P("dom", None)),
        check_vma=False,
    )
```

```python
import jax
import jax.numpy as jnp
from jax import lax
from jax.experimental import pallas as pl
from jax.experimental.pallas import tpu as pltpu
from jax.sharding import PartitionSpec as P

MESH = pl.DeviceIdType.MESH
F32 = jnp.float32
BF16 = jnp.bfloat16
DOM = 32
FREQ = 8
RIM = 256
EDGES = 1280
CHUNKS = EDGES // 128
GROUPS = 4
PARTS = 2
STACK = 8 * PARTS
HOPS = (0, 1, 2, 1)
DOM_PEERS = sorted(range(1, DOM), key=lambda k: (-HOPS[k // 8] - HOPS[k // 2 % 4], k))
FREQ_PEERS = (4, 3, 5, 2, 6, 1, 7)


def rows_iota(shape):
    return lax.broadcasted_iota(jnp.int32, shape, 0)


def lanes_iota(shape):
    return lax.broadcasted_iota(jnp.int32, shape, 1)


def lane_pick(table, lane):
    return jnp.take_along_axis(table, lane, axis=1, mode="promise_in_bounds")


def spread(row):
    return jnp.broadcast_to(row, (8, 128))


def chunk(field, c):
    return field[:, 128 * c : 128 * (c + 1)]


def field_rows(ref):
    out = jnp.broadcast_to(ref[0, 0], (8, EDGES))
    kind = rows_iota((8, EDGES)) % 4
    for v in range(1, 4):
        out = jnp.where(kind == v, jnp.broadcast_to(ref[v // 2, v % 2], (8, EDGES)), out)
    return out


def permuted(rim, order):
    out = []
    for q in range(2):
        index = chunk(order, q)
        lane = index & 127
        low = lane_pick(rim[:, :128], lane)
        high = lane_pick(rim[:, 128:], lane)
        out.append(jnp.where(index < 128, low, high))
    return jnp.concatenate(out, axis=1)


def pick(field, index):
    lane = index & 127
    found = [lane_pick(chunk(field, c), lane) for c in range(CHUNKS)]
    bit = 7
    while len(found) > 1:
        odd = (index & (1 << bit)) != 0
        merged = [jnp.where(odd, found[n + 1], found[n]) for n in range(0, len(found) - 1, 2)]
        if len(found) % 2:
            merged.append(found[-1])
        found = merged
        bit += 1
    return found[0]


def edge_dot(a, b, own=None):
    total = chunk(a, 2) * chunk(b, 2)
    for c in range(3, CHUNKS):
        total = total + chunk(a, c) * chunk(b, c)
    rim = chunk(a, 0) * chunk(b, 0) + chunk(a, 1) * chunk(b, 1)
    return total + (rim if own is None else own * rim)


def kernel(
    angular_hbm,
    stiffness_hbm,
    mass_hbm,
    conductivity_hbm,
    edges_hbm,
    live_hbm,
    source_hbm,
    forward_hbm,
    order_hbm,
    total_ref,
    angular,
    stiffness,
    mass,
    conductivity,
    edges,
    live,
    source,
    forward,
    order,
    ids,
    masks,
    onehot,
    blocks,
    weight,
    values,
    down_out,
    up_out,
    down_in,
    up_in,
    sums,
    terms,
    load_sem,
    down_send,
    down_recv,
    up_send,
    up_recv,
    sum_send,
    sum_recv,
    term_send,
    term_recv,
):
    me = lax.axis_index("dom")
    my_freq = lax.axis_index("freq")
    below = lax.rem(me + DOM - 1, DOM)
    above = lax.rem(me + 1, DOM)

    loads = [
        pltpu.make_async_copy(src, dst, load_sem.at[n])
        for n, (src, dst) in enumerate(
            [
                (source_hbm, source),
                (order_hbm, order),
                (edges_hbm, edges),
                (forward_hbm, forward),
                (stiffness_hbm, stiffness),
                (mass_hbm, mass),
                (conductivity_hbm, conductivity),
                (live_hbm, live),
                (angular_hbm, angular),
            ]
        )
    ]
    for load in loads:
        load.start()

    barrier = pltpu.get_barrier_semaphore()
    for k in DOM_PEERS:
        pl.semaphore_signal(barrier, inc=1, device_id=(my_freq, me ^ k), device_id_type=MESH)
    for k in FREQ_PEERS:
        peer = lax.rem(my_freq + k, FREQ)
        pl.semaphore_signal(barrier, inc=1, device_id=(peer, me), device_id_type=MESH)

    lane = lanes_iota((8, 128))
    sub = rows_iota((8, 128))
    upper = sub < 4

    def halves(ref, n, q):
        first = ref[n, :, pl.ds(pl.multiple_of(128 * q, 128), 128)]
        second = ref[n, :, pl.ds(pl.multiple_of(512 + 128 * q, 128), 128)]
        return jnp.where(upper, spread(first), spread(second))

    loads[0].wait()
    loads[1].wait()
    order_rows = jnp.broadcast_to(order[...], (8, RIM))
    match = jnp.where(rows_iota((RIM, RIM)) == jnp.broadcast_to(order[...], (RIM, RIM)), 1.0, 0.0)
    inverse = lax.dot_general(
        lanes_iota((8, RIM)).astype(F32).astype(BF16),
        match.astype(BF16),
        (((1,), (1,)), ((), ())),
        preferred_element_type=F32,
    ).astype(jnp.int32)
    sources = field_rows(source)

    loads[2].wait()

    def tables(q, carry):
        for i in range(6):
            index = halves(edges, i, q)
            ids[q, i] = index
            wide = index >> 7
            for c in range(CHUNKS):
                hit = jnp.where(wide == c, 1.0, 0.0)
                masks[q, c, :, 128 * i : 128 * (i + 1)] = jnp.concatenate([hit] * PARTS, axis=0).astype(BF16)
        for h in range(2):
            at = pl.ds(pl.multiple_of(512 * h + 128 * q, 128), 128)
            stacked = spread(edges[0, :, at])
            for i in range(1, 6):
                stacked = jnp.where(sub == i, spread(edges[i, :, at]), stacked)
            columns = jnp.transpose(stacked & 127)
            for i in range(6):
                hit = jnp.broadcast_to(columns[:, i : i + 1], (128, 128)) == lanes_iota((128, 128))
                onehot[q, 128 * i : 128 * (i + 1), 128 * h : 128 * (h + 1)] = jnp.where(hit, 1.0, 0.0).astype(BF16)
        return carry

    lax.fori_loop(0, GROUPS, tables, 0)

    @pl.when(me == 0)
    def _():
        up_in[...] = jnp.zeros((3, 8, RIM), F32)

    @pl.when(me == DOM - 1)
    def _():
        down_in[...] = jnp.zeros((3, 8, RIM), F32)

    def send_rims(k, field):
        down_out[k] = permuted(field[:, :RIM], inverse)
        up_out[k] = field[:, EDGES - RIM :]
        copies = (
            pltpu.make_async_remote_copy(
                src_ref=down_out.at[k],
                dst_ref=down_in.at[k],
                send_sem=down_send.at[k],
                recv_sem=down_recv.at[k],
                device_id=(my_freq, below),
                device_id_type=MESH,
            ),
            pltpu.make_async_remote_copy(
                src_ref=up_out.at[k],
                dst_ref=up_in.at[k],
                send_sem=up_send.at[k],
                recv_sem=up_recv.at[k],
                device_id=(my_freq, above),
                device_id_type=MESH,
            ),
        )
        pl.when(me > 0)(copies[0].start)
        pl.when(me < DOM - 1)(copies[1].start)
        return copies

    def join_rims(k, copies, field):
        pl.when(me < DOM - 1)(copies[0].wait_recv)
        pl.when(me > 0)(copies[1].wait_recv)
        return jnp.concatenate(
            [
                field[:, :RIM] + permuted(up_in[k], order_rows),
                field[:, RIM : EDGES - RIM],
                field[:, EDGES - RIM :] + down_in[k],
            ],
            axis=1,
        )

    pl.semaphore_wait(barrier, DOM - 1 + FREQ - 1)
    rims0 = send_rims(0, sources)

    for n in range(3, 9):
        loads[n].wait()
    omega = jnp.where(sub % 4 < 2, angular[0], angular[1])
    forwards = field_rows(forward)

    def elements(q, carry):
        alive = halves(live, 0, q).astype(F32)
        shift = omega * (halves(conductivity, 0, q) * alive)
        picked = [pick(forwards, ids[q, j]) for j in range(6)]
        for i in range(6):
            running = None
            for j in range(6):
                n = 6 * i + j
                mass_rows = halves(mass, n, q)
                blocks[q, n] = halves(stiffness, n, q) * alive + shift * mass_rows
                product = mass_rows * picked[j]
                running = product if running is None else running + product
            weight[q, i] = omega * running
        return carry

    lax.fori_loop(0, GROUPS, elements, 0)

    def apply(field):
        out = None
        terms_of = []
        for q in range(GROUPS):
            picked = [pick(field, ids[q, i]) for i in range(6)]
            term = weight[q, 0] * picked[0]
            for i in range(1, 6):
                term = term + weight[q, i] * picked[i]
            terms_of.append(term)
            for i in range(6):
                running = blocks[q, 6 * i] * picked[0]
                for j in range(1, 6):
                    running = running + blocks[q, 6 * i + j] * picked[j]
                pieces = []
                rest = running
                for _ in range(PARTS - 1):
                    head = rest.astype(BF16).astype(F32)
                    pieces.append(head)
                    rest = rest - head
                pieces.append(rest)
                stacked = jnp.concatenate(pieces, axis=0).astype(BF16)
                for c in range(CHUNKS):
                    values[q, STACK * c : STACK * (c + 1), 128 * i : 128 * (i + 1)] = (
                        stacked * masks[q, c, :, 128 * i : 128 * (i + 1)]
                    )
            product = lax.dot_general(
                values[q], onehot[q], (((1,), (0,)), ((), ())), preferred_element_type=F32
            )
            out = product if out is None else out + product
        pieces = []
        for c in range(CHUNKS):
            both = out[STACK * c : STACK * c + 8]
            for s in range(1, PARTS):
                both = both + out[STACK * c + 8 * s : STACK * c + 8 * s + 8]
            mixed = jnp.where(upper, both[:, :128], both[:, 128:])
            pieces.append(mixed + pltpu.roll(mixed, 4, 0))
        return jnp.concatenate(pieces, axis=1), jnp.concatenate(terms_of, axis=1)

    def send_sums(k, quantities):
        row = jnp.zeros((8, 128), F32)
        for n, quantity in enumerate(quantities):
            column = jnp.sum(quantity, axis=1, keepdims=True)
            row = row + jnp.where((lane == 4 * n + sub) & upper, column, 0.0)
        sums[k, me] = jnp.sum(row, axis=0, keepdims=True)
        for n in DOM_PEERS:
            pltpu.make_async_remote_copy(
                src_ref=sums.at[k, me],
                dst_ref=sums.at[k, me],
                send_sem=sum_send.at[k],
                recv_sem=sum_recv.at[k],
                device_id=(my_freq, me ^ n),
                device_id_type=MESH,
            ).start()

    def take_sums(k, count):
        rest = sums.at[k, pl.ds(0, DOM - 1)]
        pltpu.make_async_copy(rest, rest, sum_recv.at[k]).wait()
        total = spread(jnp.sum(sums[k], axis=0))
        return [
            jnp.sum(jnp.where(lane == 4 * n + sub % 4, total, 0.0), axis=1, keepdims=True)
            for n in range(count)
        ]

    own = jnp.where(me > 0, 0.0, 1.0).astype(F32)

    base = join_rims(0, rims0, sources)
    image0, term0 = apply(base)
    rims1 = send_rims(1, image0)
    send_sums(0, [edge_dot(base, base, own), edge_dot(base, image0)])
    first = join_rims(1, rims1, image0)
    image1, term1 = apply(first)
    rims2 = send_rims(2, image1)

    norm0, curve0 = take_sums(0, 2)
    alpha0 = norm0 / curve0
    residual = base - alpha0 * first
    residual_image = image0 - alpha0 * image1
    early = [
        edge_dot(residual, residual, own),
        edge_dot(residual, residual_image),
        edge_dot(base, residual_image),
        edge_dot(first, first, own),
        edge_dot(first, image1),
    ]
    near = term0 - alpha0 * term1
    second = join_rims(2, rims2, image1)
    turned = first - alpha0 * second
    early += [edge_dot(turned, turned, own), edge_dot(first, turned, own)]
    image2, term2 = apply(second)
    turned_image = image1 - alpha0 * image2
    send_sums(1, early + [edge_dot(turned, turned_image), edge_dot(first, turned_image)])
    far = term1 - alpha0 * term2

    norm1, rr1, br1, bb2, bb3, rr2, br2, rr3, br3 = take_sums(1, 9)
    beta0 = norm1 / norm0
    along1 = rr1 + beta0 * br1
    curve1 = along1 + beta0 * (br1 + beta0 * curve0)
    alpha1 = norm1 / curve1
    square = rr2 + beta0 * (2.0 * br2 + beta0 * bb2)
    norm2 = norm1 - alpha1 * (2.0 * along1 - alpha1 * square)
    self2 = rr1 - alpha1 * (2.0 * (rr2 + beta0 * br2) - alpha1 * (rr3 + beta0 * (2.0 * br3 + beta0 * bb3)))
    cross2 = along1 - alpha1 * square
    beta1 = norm2 / norm1
    curve2 = self2 + beta1 * (2.0 * cross2 + beta1 * curve1)
    alpha2 = norm2 / curve2
    on_d1 = alpha1 + alpha2 * beta1
    total = (
        (alpha0 + on_d1 * beta0) * term0
        + (on_d1 + alpha2) * near
        - (alpha2 * alpha1) * (far + beta0 * term1)
    )

    total = total + pltpu.roll(total, 1, 0)
    total = total + pltpu.roll(total, 2, 0)
    packed = jnp.zeros((8, 128), F32)
    for h in range(2):
        for q in range(GROUPS):
            piece = spread(total[4 * h + 3 : 4 * h + 4, 128 * q : 128 * (q + 1)])
            packed = jnp.where(sub == 4 * h + q, piece, packed)
    terms[my_freq] = packed
    for n in FREQ_PEERS:
        peer = lax.rem(my_freq + n, FREQ)
        pltpu.make_async_remote_copy(
            src_ref=terms.at[my_freq],
            dst_ref=terms.at[my_freq],
            send_sem=term_send,
            recv_sem=term_recv,
            device_id=(peer, me),
            device_id_type=MESH,
        ).start()
    for copies in (rims0, rims1, rims2):
        pl.when(me > 0)(copies[0].wait_send)
        pl.when(me < DOM - 1)(copies[1].wait_send)
    for k in range(2):
        sent = sums.at[k, pl.ds(0, DOM - 1)]
        pltpu.make_async_copy(sent, sent, sum_send.at[k]).wait()
    rest = terms.at[pl.ds(0, FREQ - 1)]
    pltpu.make_async_copy(rest, rest, term_recv).wait()
    added = terms[0]
    for n in range(1, FREQ):
        added = added + terms[n]
    for r in range(8):
        total_ref[:, 128 * r : 128 * (r + 1)] = added[r : r + 1]
    pltpu.make_async_copy(rest, rest, term_send).wait()


def local(
    angular,
    stiffness,
    mass_matrix,
    conductivity,
    element_edges,
    live_slots,
    adjoint_source,
    forward_field,
    neighbour_map,
):
    hbm = pl.BlockSpec(memory_space=pltpu.MemorySpace.HBM)
    dma = pltpu.SemaphoreType.DMA
    total = pl.pallas_call(
        kernel,
        out_shape=jax.ShapeDtypeStruct((1, 1024), F32),
        in_specs=[hbm] * 9,
        out_specs=pl.BlockSpec(memory_space=pltpu.MemorySpace.VMEM),
        scratch_shapes=[
            pltpu.SMEM((2,), F32),
            pltpu.VMEM((36, 1, 1024), F32),
            pltpu.VMEM((36, 1, 1024), F32),
            pltpu.VMEM((1, 1, 1024), F32),
            pltpu.VMEM((6, 1, 1024), jnp.int32),
            pltpu.VMEM((1, 1, 1024), jnp.int32),
            pltpu.VMEM((2, 2, 1, EDGES), F32),
            pltpu.VMEM((2, 2, 1, EDGES), F32),
            pltpu.VMEM((1, RIM), jnp.int32),
            pltpu.VMEM((GROUPS, 6, 8, 128), jnp.int32),
            pltpu.VMEM((GROUPS, CHUNKS, STACK, 768), BF16),
            pltpu.VMEM((GROUPS, 768, 256), BF16),
            pltpu.VMEM((GROUPS, 36, 8, 128), F32),
            pltpu.VMEM((GROUPS, 6, 8, 128), F32),
            pltpu.VMEM((GROUPS, STACK * CHUNKS, 768), BF16),
            pltpu.VMEM((3, 8, RIM), F32),
            pltpu.VMEM((3, 8, RIM), F32),
            pltpu.VMEM((3, 8, RIM), F32),
            pltpu.VMEM((3, 8, RIM), F32),
            pltpu.VMEM((2, DOM, 1, 128), F32),
            pltpu.VMEM((FREQ, 8, 128), F32),
            dma((9,)),
            dma((3,)),
            dma((3,)),
            dma((3,)),
            dma((3,)),
            dma((3,)),
            dma((3,)),
            dma,
            dma,
        ],
        compiler_params=pltpu.CompilerParams(collective_id=0, has_side_effects=True),
    )(
        angular,
        jnp.transpose(stiffness, (1, 0, 2)),
        jnp.transpose(mass_matrix, (1, 0, 2)),
        conductivity[None],
        jnp.transpose(element_edges, (1, 0, 2)),
        live_slots[None],
        adjoint_source,
        forward_field,
        neighbour_map,
    )
    gradient = -total * live_slots.astype(F32)
    updated = conductivity * jnp.exp(-0.5 * jnp.tanh(gradient))
    return gradient, updated


def solution(mesh):
    return jax.shard_map(
        local,
        mesh=mesh,
        in_specs=(
            P("freq"),
            P("dom", None, None),
            P("dom", None, None),
            P("dom", None),
            P("dom", None, None),
            P("dom", None),
            P("freq", None, "dom", None),
            P("freq", None, "dom", None),
            P("dom", None),
        ),
        out_specs=(P("dom", None), P("dom", None)),
        check_vma=False,
    )
```

```python
import jax
import jax.numpy as jnp
from jax import lax
from jax.experimental import pallas as pl
from jax.experimental.pallas import tpu as pltpu
from jax.sharding import PartitionSpec as P

MESH = pl.DeviceIdType.MESH
F32 = jnp.float32
BF16 = jnp.bfloat16
DOM = 32
FREQ = 8
RIM = 256
EDGES = 1280
CHUNKS = EDGES // 128
GROUPS = 4
PARTS = 2
STACK = 8 * PARTS
HOPS = (0, 1, 2, 1)
DOM_PEERS = sorted(range(1, DOM), key=lambda k: (-HOPS[k // 8] - HOPS[k // 2 % 4], k))
FREQ_PEERS = (4, 3, 5, 2, 6, 1, 7)
NEAR = [k for k in range(1, DOM) if HOPS[k // 8] + HOPS[k // 2 % 4] <= 1]
ONE_HOP = [k for k in NEAR if k % 2 == 0]
TWO_HOPS = [k for k in range(0, DOM, 2) if HOPS[k // 8] + HOPS[k // 2 % 4] == 2]


def rows_iota(shape):
    return lax.broadcasted_iota(jnp.int32, shape, 0)


def lanes_iota(shape):
    return lax.broadcasted_iota(jnp.int32, shape, 1)


def lane_pick(table, lane):
    return jnp.take_along_axis(table, lane, axis=1, mode="promise_in_bounds")


def spread(row):
    return jnp.broadcast_to(row, (8, 128))


def chunk(field, c):
    return field[:, 128 * c : 128 * (c + 1)]


def field_rows(ref):
    out = jnp.broadcast_to(ref[0, 0], (8, EDGES))
    kind = rows_iota((8, EDGES)) % 4
    for v in range(1, 4):
        out = jnp.where(kind == v, jnp.broadcast_to(ref[v // 2, v % 2], (8, EDGES)), out)
    return out


def permuted(rim, order):
    out = []
    for q in range(2):
        index = chunk(order, q)
        lane = index & 127
        low = lane_pick(rim[:, :128], lane)
        high = lane_pick(rim[:, 128:], lane)
        out.append(jnp.where(index < 128, low, high))
    return jnp.concatenate(out, axis=1)


def pick(field, index):
    lane = index & 127
    found = [lane_pick(chunk(field, c), lane) for c in range(CHUNKS)]
    bit = 7
    while len(found) > 1:
        odd = (index & (1 << bit)) != 0
        merged = [jnp.where(odd, found[n + 1], found[n]) for n in range(0, len(found) - 1, 2)]
        if len(found) % 2:
            merged.append(found[-1])
        found = merged
        bit += 1
    return found[0]


def edge_dot(a, b, own=None):
    total = chunk(a, 2) * chunk(b, 2)
    for c in range(3, CHUNKS):
        total = total + chunk(a, c) * chunk(b, c)
    rim = chunk(a, 0) * chunk(b, 0) + chunk(a, 1) * chunk(b, 1)
    return total + (rim if own is None else own * rim)


def kernel(
    angular_hbm,
    stiffness_hbm,
    mass_hbm,
    conductivity_hbm,
    edges_hbm,
    live_hbm,
    source_hbm,
    forward_hbm,
    order_hbm,
    total_ref,
    angular,
    stiffness,
    mass,
    conductivity,
    edges,
    live,
    source,
    forward,
    order,
    ids,
    masks,
    onehot,
    blocks,
    weight,
    values,
    down_out,
    up_out,
    down_in,
    up_in,
    sums,
    terms,
    load_sem,
    down_send,
    down_recv,
    up_send,
    up_recv,
    sum_send,
    sum_recv,
    term_send,
    term_recv,
    round_two,
    round_three,
):
    me = lax.axis_index("dom")
    my_freq = lax.axis_index("freq")
    below = lax.rem(me + DOM - 1, DOM)
    above = lax.rem(me + 1, DOM)

    loads = [
        pltpu.make_async_copy(src, dst, load_sem.at[n])
        for n, (src, dst) in enumerate(
            [
                (source_hbm, source),
                (order_hbm, order),
                (edges_hbm, edges),
                (forward_hbm, forward),
                (stiffness_hbm, stiffness),
                (mass_hbm, mass),
                (conductivity_hbm, conductivity),
                (live_hbm, live),
                (angular_hbm, angular),
            ]
        )
    ]
    for load in loads:
        load.start()

    barrier = pltpu.get_barrier_semaphore()
    row_end = lax.rem(me, 8) == 7
    row_start = lax.rem(me, 8) == 0
    end_pair = row_end & (me < DOM - 1)
    start_pair = row_start & (me > 0)

    def signal(semaphore, freq, dom):
        pl.semaphore_signal(semaphore, inc=1, device_id=(freq, dom), device_id_type=MESH)

    pl.when(end_pair)(lambda: signal(barrier, my_freq, above))
    pl.when(start_pair)(lambda: signal(barrier, my_freq, below))
    for k in NEAR:
        signal(barrier, my_freq, me ^ k)
    for d in (1, 7):
        signal(barrier, lax.rem(my_freq + d, FREQ), me)

    lane = lanes_iota((8, 128))
    sub = rows_iota((8, 128))
    upper = sub < 4

    def halves(ref, n, q):
        first = ref[n, :, pl.ds(pl.multiple_of(128 * q, 128), 128)]
        second = ref[n, :, pl.ds(pl.multiple_of(512 + 128 * q, 128), 128)]
        return jnp.where(upper, spread(first), spread(second))

    loads[0].wait()
    loads[1].wait()
    order_rows = jnp.broadcast_to(order[...], (8, RIM))
    match = jnp.where(rows_iota((RIM, RIM)) == jnp.broadcast_to(order[...], (RIM, RIM)), 1.0, 0.0)
    inverse = lax.dot_general(
        lanes_iota((8, RIM)).astype(F32).astype(BF16),
        match.astype(BF16),
        (((1,), (1,)), ((), ())),
        preferred_element_type=F32,
    ).astype(jnp.int32)
    sources = field_rows(source)

    @pl.when(me == 0)
    def _():
        up_in[...] = jnp.zeros((3, 8, RIM), F32)

    @pl.when(me == DOM - 1)
    def _():
        down_in[...] = jnp.zeros((3, 8, RIM), F32)

    def send_rims(k, field):
        down_out[k] = permuted(field[:, :RIM], inverse)
        up_out[k] = field[:, EDGES - RIM :]
        copies = (
            pltpu.make_async_remote_copy(
                src_ref=down_out.at[k],
                dst_ref=down_in.at[k],
                send_sem=down_send.at[k],
                recv_sem=down_recv.at[k],
                device_id=(my_freq, below),
                device_id_type=MESH,
            ),
            pltpu.make_async_remote_copy(
                src_ref=up_out.at[k],
                dst_ref=up_in.at[k],
                send_sem=up_send.at[k],
                recv_sem=up_recv.at[k],
                device_id=(my_freq, above),
                device_id_type=MESH,
            ),
        )
        pl.when(me > 0)(copies[0].start)
        pl.when(me < DOM - 1)(copies[1].start)
        return copies

    def join_rims(k, copies, field):
        pl.when(me < DOM - 1)(copies[0].wait_recv)
        pl.when(me > 0)(copies[1].wait_recv)
        return jnp.concatenate(
            [
                field[:, :RIM] + permuted(up_in[k], order_rows),
                field[:, RIM : EDGES - RIM],
                field[:, EDGES - RIM :] + down_in[k],
            ],
            axis=1,
        )

    pl.semaphore_wait(barrier, len(NEAR) + 2 + end_pair.astype(jnp.int32) + start_pair.astype(jnp.int32))
    rims0 = send_rims(0, sources)
    for k in ONE_HOP:
        signal(round_two, my_freq, me ^ k)
    for d in (1, 7):
        signal(round_two, lax.rem(my_freq + d, FREQ), me)

    loads[2].wait()

    def tables(q, carry):
        for i in range(6):
            index = halves(edges, i, q)
            ids[q, i] = index
            wide = index >> 7
            for c in range(CHUNKS):
                hit = jnp.where(wide == c, 1.0, 0.0)
                masks[q, c, :, 128 * i : 128 * (i + 1)] = jnp.concatenate([hit] * PARTS, axis=0).astype(BF16)
        for h in range(2):
            at = pl.ds(pl.multiple_of(512 * h + 128 * q, 128), 128)
            stacked = spread(edges[0, :, at])
            for i in range(1, 6):
                stacked = jnp.where(sub == i, spread(edges[i, :, at]), stacked)
            columns = jnp.transpose(stacked & 127)
            for i in range(6):
                hit = jnp.broadcast_to(columns[:, i : i + 1], (128, 128)) == lanes_iota((128, 128))
                onehot[q, 128 * i : 128 * (i + 1), 128 * h : 128 * (h + 1)] = jnp.where(hit, 1.0, 0.0).astype(BF16)
        return carry

    lax.fori_loop(0, GROUPS, tables, 0)

    for n in range(3, 9):
        loads[n].wait()
    omega = jnp.where(sub % 4 < 2, angular[0], angular[1])
    forwards = field_rows(forward)

    def elements(q, carry):
        alive = halves(live, 0, q).astype(F32)
        shift = omega * (halves(conductivity, 0, q) * alive)
        picked = [pick(forwards, ids[q, j]) for j in range(6)]
        for i in range(6):
            running = None
            for j in range(6):
                n = 6 * i + j
                mass_rows = halves(mass, n, q)
                blocks[q, n] = halves(stiffness, n, q) * alive + shift * mass_rows
                product = mass_rows * picked[j]
                running = product if running is None else running + product
            weight[q, i] = omega * running
        return carry

    lax.fori_loop(0, GROUPS, elements, 0)

    pl.semaphore_wait(round_two, len(ONE_HOP) + 2)
    for k in TWO_HOPS:
        signal(round_three, my_freq, me ^ k)
    for d in (2, 6):
        signal(round_three, lax.rem(my_freq + d, FREQ), me)

    def apply(field):
        out = None
        terms_of = []
        for q in range(GROUPS):
            picked = [pick(field, ids[q, i]) for i in range(6)]
            term = weight[q, 0] * picked[0]
            for i in range(1, 6):
                term = term + weight[q, i] * picked[i]
            terms_of.append(term)
            for i in range(6):
                running = blocks[q, 6 * i] * picked[0]
                for j in range(1, 6):
                    running = running + blocks[q, 6 * i + j] * picked[j]
                pieces = []
                rest = running
                for _ in range(PARTS - 1):
                    head = rest.astype(BF16).astype(F32)
                    pieces.append(head)
                    rest = rest - head
                pieces.append(rest)
                stacked = jnp.concatenate(pieces, axis=0).astype(BF16)
                for c in range(CHUNKS):
                    values[q, STACK * c : STACK * (c + 1), 128 * i : 128 * (i + 1)] = (
                        stacked * masks[q, c, :, 128 * i : 128 * (i + 1)]
                    )
            product = lax.dot_general(
                values[q], onehot[q], (((1,), (0,)), ((), ())), preferred_element_type=F32
            )
            out = product if out is None else out + product
        pieces = []
        for c in range(CHUNKS):
            both = out[STACK * c : STACK * c + 8]
            for s in range(1, PARTS):
                both = both + out[STACK * c + 8 * s : STACK * c + 8 * s + 8]
            mixed = jnp.where(upper, both[:, :128], both[:, 128:])
            pieces.append(mixed + pltpu.roll(mixed, 4, 0))
        return jnp.concatenate(pieces, axis=1), jnp.concatenate(terms_of, axis=1)

    def send_sums(k, quantities):
        row = jnp.zeros((8, 128), F32)
        for n, quantity in enumerate(quantities):
            column = jnp.sum(quantity, axis=1, keepdims=True)
            row = row + jnp.where((lane == 4 * n + sub) & upper, column, 0.0)
        sums[k, me] = jnp.sum(row, axis=0, keepdims=True)
        for n in DOM_PEERS:
            pltpu.make_async_remote_copy(
                src_ref=sums.at[k, me],
                dst_ref=sums.at[k, me],
                send_sem=sum_send.at[k],
                recv_sem=sum_recv.at[k],
                device_id=(my_freq, me ^ n),
                device_id_type=MESH,
            ).start()

    def take_sums(k, count):
        rest = sums.at[k, pl.ds(0, DOM - 1)]
        pltpu.make_async_copy(rest, rest, sum_recv.at[k]).wait()
        total = spread(jnp.sum(sums[k], axis=0))
        return [
            jnp.sum(jnp.where(lane == 4 * n + sub % 4, total, 0.0), axis=1, keepdims=True)
            for n in range(count)
        ]

    own = jnp.where(me > 0, 0.0, 1.0).astype(F32)

    base = join_rims(0, rims0, sources)
    image0, term0 = apply(base)
    rims1 = send_rims(1, image0)
    first = join_rims(1, rims1, image0)
    pl.semaphore_wait(round_three, len(TWO_HOPS) + 2)
    send_sums(0, [edge_dot(base, base, own), edge_dot(base, image0)])
    image1, term1 = apply(first)
    rims2 = send_rims(2, image1)

    second = join_rims(2, rims2, image1)
    image2, term2 = apply(second)

    norm0, curve0 = take_sums(0, 2)
    alpha0 = norm0 / curve0
    residual = base - alpha0 * first
    residual_image = image0 - alpha0 * image1
    turned = first - alpha0 * second
    turned_image = image1 - alpha0 * image2
    send_sums(
        1,
        [
            edge_dot(residual, residual, own),
            edge_dot(residual, residual_image),
            edge_dot(base, residual_image),
            edge_dot(first, first, own),
            edge_dot(first, image1),
            edge_dot(turned, turned, own),
            edge_dot(first, turned, own),
            edge_dot(turned, turned_image),
            edge_dot(first, turned_image),
        ],
    )
    near = term0 - alpha0 * term1
    far = term1 - alpha0 * term2

    norm1, rr1, br1, bb2, bb3, rr2, br2, rr3, br3 = take_sums(1, 9)
    beta0 = norm1 / norm0
    along1 = rr1 + beta0 * br1
    curve1 = along1 + beta0 * (br1 + beta0 * curve0)
    alpha1 = norm1 / curve1
    square = rr2 + beta0 * (2.0 * br2 + beta0 * bb2)
    norm2 = norm1 - alpha1 * (2.0 * along1 - alpha1 * square)
    self2 = rr1 - alpha1 * (2.0 * (rr2 + beta0 * br2) - alpha1 * (rr3 + beta0 * (2.0 * br3 + beta0 * bb3)))
    cross2 = along1 - alpha1 * square
    beta1 = norm2 / norm1
    curve2 = self2 + beta1 * (2.0 * cross2 + beta1 * curve1)
    alpha2 = norm2 / curve2
    on_d1 = alpha1 + alpha2 * beta1
    total = (
        (alpha0 + on_d1 * beta0) * term0
        + (on_d1 + alpha2) * near
        - (alpha2 * alpha1) * (far + beta0 * term1)
    )

    total = total + pltpu.roll(total, 1, 0)
    total = total + pltpu.roll(total, 2, 0)
    packed = jnp.zeros((8, 128), F32)
    for h in range(2):
        for q in range(GROUPS):
            piece = spread(total[4 * h + 3 : 4 * h + 4, 128 * q : 128 * (q + 1)])
            packed = jnp.where(sub == 4 * h + q, piece, packed)
    terms[my_freq] = packed
    for n in FREQ_PEERS:
        peer = lax.rem(my_freq + n, FREQ)
        pltpu.make_async_remote_copy(
            src_ref=terms.at[my_freq],
            dst_ref=terms.at[my_freq],
            send_sem=term_send,
            recv_sem=term_recv,
            device_id=(peer, me),
            device_id_type=MESH,
        ).start()
    for copies in (rims0, rims1, rims2):
        pl.when(me > 0)(copies[0].wait_send)
        pl.when(me < DOM - 1)(copies[1].wait_send)
    for k in range(2):
        sent = sums.at[k, pl.ds(0, DOM - 1)]
        pltpu.make_async_copy(sent, sent, sum_send.at[k]).wait()
    rest = terms.at[pl.ds(0, FREQ - 1)]
    pltpu.make_async_copy(rest, rest, term_recv).wait()
    added = terms[0]
    for n in range(1, FREQ):
        added = added + terms[n]
    for r in range(8):
        total_ref[:, 128 * r : 128 * (r + 1)] = added[r : r + 1]
    pltpu.make_async_copy(rest, rest, term_send).wait()


def local(
    angular,
    stiffness,
    mass_matrix,
    conductivity,
    element_edges,
    live_slots,
    adjoint_source,
    forward_field,
    neighbour_map,
):
    hbm = pl.BlockSpec(memory_space=pltpu.MemorySpace.HBM)
    dma = pltpu.SemaphoreType.DMA
    total = pl.pallas_call(
        kernel,
        out_shape=pltpu.VMEM((1, 1024), F32),
        in_specs=[hbm] * 9,
        out_specs=pl.BlockSpec(memory_space=pltpu.MemorySpace.VMEM),
        scratch_shapes=[
            pltpu.SMEM((2,), F32),
            pltpu.VMEM((36, 1, 1024), F32),
            pltpu.VMEM((36, 1, 1024), F32),
            pltpu.VMEM((1, 1, 1024), F32),
            pltpu.VMEM((6, 1, 1024), jnp.int32),
            pltpu.VMEM((1, 1, 1024), jnp.int32),
            pltpu.VMEM((2, 2, 1, EDGES), F32),
            pltpu.VMEM((2, 2, 1, EDGES), F32),
            pltpu.VMEM((1, RIM), jnp.int32),
            pltpu.VMEM((GROUPS, 6, 8, 128), jnp.int32),
            pltpu.VMEM((GROUPS, CHUNKS, STACK, 768), BF16),
            pltpu.VMEM((GROUPS, 768, 256), BF16),
            pltpu.VMEM((GROUPS, 36, 8, 128), F32),
            pltpu.VMEM((GROUPS, 6, 8, 128), F32),
            pltpu.VMEM((GROUPS, STACK * CHUNKS, 768), BF16),
            pltpu.VMEM((3, 8, RIM), F32),
            pltpu.VMEM((3, 8, RIM), F32),
            pltpu.VMEM((3, 8, RIM), F32),
            pltpu.VMEM((3, 8, RIM), F32),
            pltpu.VMEM((2, DOM, 1, 128), F32),
            pltpu.VMEM((FREQ, 8, 128), F32),
            dma((9,)),
            dma((3,)),
            dma((3,)),
            dma((3,)),
            dma((3,)),
            dma((3,)),
            dma((3,)),
            dma,
            dma,
            pltpu.SemaphoreType.REGULAR,
            pltpu.SemaphoreType.REGULAR,
        ],
        compiler_params=pltpu.CompilerParams(collective_id=0, has_side_effects=True),
    )(
        angular,
        jnp.transpose(stiffness, (1, 0, 2)),
        jnp.transpose(mass_matrix, (1, 0, 2)),
        conductivity[None],
        jnp.transpose(element_edges, (1, 0, 2)),
        live_slots[None],
        adjoint_source,
        forward_field,
        neighbour_map,
    )
    gradient = -total * live_slots.astype(F32)
    updated = conductivity * jnp.exp(-0.5 * jnp.tanh(gradient))
    return gradient, updated


def solution(mesh):
    return jax.shard_map(
        local,
        mesh=mesh,
        in_specs=(
            P("freq"),
            P("dom", None, None),
            P("dom", None, None),
            P("dom", None),
            P("dom", None, None),
            P("dom", None),
            P("freq", None, "dom", None),
            P("freq", None, "dom", None),
            P("dom", None),
        ),
        out_specs=(P("dom", None), P("dom", None)),
        check_vma=False,
    )
```

```python
import jax
import jax.numpy as jnp
from jax import lax
from jax.experimental import pallas as pl
from jax.experimental.pallas import tpu as pltpu
from jax.sharding import PartitionSpec as P

MESH = pl.DeviceIdType.MESH
F32 = jnp.float32
BF16 = jnp.bfloat16
DOM = 32
FREQ = 8
RIM = 256
EDGES = 1280
CHUNKS = EDGES // 128
GROUPS = 4
WIDE = EDGES // RIM
PARTS = 2
STACK = 8 * PARTS
HOPS = (0, 1, 2, 1)
DOM_PEERS = sorted(range(1, DOM), key=lambda k: (-HOPS[k // 8] - HOPS[k // 2 % 4], k))
FREQ_PEERS = (4, 3, 5, 2, 6, 1, 7)
NEAR = [k for k in range(1, DOM) if HOPS[k // 8] + HOPS[k // 2 % 4] <= 1]
ONE_HOP = [k for k in NEAR if k % 2 == 0]
TWO_HOPS = [k for k in range(0, DOM, 2) if HOPS[k // 8] + HOPS[k // 2 % 4] == 2]


def rows_iota(shape):
    return lax.broadcasted_iota(jnp.int32, shape, 0)


def lanes_iota(shape):
    return lax.broadcasted_iota(jnp.int32, shape, 1)


def lane_pick(table, lane):
    return jnp.take_along_axis(table, lane, axis=1, mode="promise_in_bounds")


def spread(row):
    return jnp.broadcast_to(row, (8, 128))


def chunk(field, c):
    return field[:, 128 * c : 128 * (c + 1)]


def field_rows(ref):
    out = jnp.broadcast_to(ref[0, 0], (8, EDGES))
    kind = rows_iota((8, EDGES)) % 4
    for v in range(1, 4):
        out = jnp.where(kind == v, jnp.broadcast_to(ref[v // 2, v % 2], (8, EDGES)), out)
    return out


def permuted(rim, order):
    out = []
    for q in range(2):
        index = chunk(order, q)
        lane = index & 127
        low = lane_pick(rim[:, :128], lane)
        high = lane_pick(rim[:, 128:], lane)
        out.append(jnp.where(index < 128, low, high))
    return jnp.concatenate(out, axis=1)


def pick(field, index):
    lane = index & 127
    found = [lane_pick(chunk(field, c), lane) for c in range(CHUNKS)]
    bit = 7
    while len(found) > 1:
        odd = (index & (1 << bit)) != 0
        merged = [jnp.where(odd, found[n + 1], found[n]) for n in range(0, len(found) - 1, 2)]
        if len(found) % 2:
            merged.append(found[-1])
        found = merged
        bit += 1
    return found[0]


def pick_rims(low, high, index):
    lane = index & 127
    odd = (index & 128) != 0
    wide = index >> 8
    first = jnp.where(odd, lane_pick(low[:, 128:], lane), lane_pick(low[:, :128], lane))
    last = jnp.where(odd, lane_pick(high[:, 128:], lane), lane_pick(high[:, :128], lane))
    return jnp.where(wide == 0, first, jnp.where(wide == WIDE - 1, last, 0.0))


def edge_dot(a, b, own=None):
    total = chunk(a, 2) * chunk(b, 2)
    for c in range(3, CHUNKS):
        total = total + chunk(a, c) * chunk(b, c)
    rim = chunk(a, 0) * chunk(b, 0) + chunk(a, 1) * chunk(b, 1)
    return total + (rim if own is None else own * rim)


def kernel(
    angular_hbm,
    stiffness_hbm,
    mass_hbm,
    conductivity_hbm,
    edges_hbm,
    live_hbm,
    source_hbm,
    forward_hbm,
    order_hbm,
    total_ref,
    angular,
    stiffness,
    mass,
    conductivity,
    edges,
    live,
    source,
    forward,
    order,
    ids,
    masks,
    onehot,
    blocks,
    weight,
    down_out,
    up_out,
    down_in,
    up_in,
    sums,
    terms,
    load_sem,
    down_send,
    down_recv,
    up_send,
    up_recv,
    sum_send,
    sum_recv,
    term_send,
    term_recv,
    round_two,
    round_three,
):
    me = lax.axis_index("dom")
    my_freq = lax.axis_index("freq")
    below = lax.rem(me + DOM - 1, DOM)
    above = lax.rem(me + 1, DOM)

    loads = [
        pltpu.make_async_copy(src, dst, load_sem.at[n])
        for n, (src, dst) in enumerate(
            [
                (source_hbm, source),
                (order_hbm, order),
                (edges_hbm, edges),
                (forward_hbm, forward),
                (stiffness_hbm, stiffness),
                (mass_hbm, mass),
                (conductivity_hbm, conductivity),
                (live_hbm, live),
                (angular_hbm, angular),
            ]
        )
    ]
    for load in loads:
        load.start()

    barrier = pltpu.get_barrier_semaphore()
    row_end = lax.rem(me, 8) == 7
    row_start = lax.rem(me, 8) == 0
    end_pair = row_end & (me < DOM - 1)
    start_pair = row_start & (me > 0)

    def signal(semaphore, freq, dom):
        pl.semaphore_signal(semaphore, inc=1, device_id=(freq, dom), device_id_type=MESH)

    pl.when(end_pair)(lambda: signal(barrier, my_freq, above))
    pl.when(start_pair)(lambda: signal(barrier, my_freq, below))
    for k in NEAR:
        signal(barrier, my_freq, me ^ k)
    for d in (1, 7):
        signal(barrier, lax.rem(my_freq + d, FREQ), me)

    lane = lanes_iota((8, 128))
    sub = rows_iota((8, 128))
    upper = sub < 4

    def halves(ref, n, q):
        first = ref[n, :, pl.ds(pl.multiple_of(128 * q, 128), 128)]
        second = ref[n, :, pl.ds(pl.multiple_of(512 + 128 * q, 128), 128)]
        return jnp.where(upper, spread(first), spread(second))

    loads[0].wait()
    loads[1].wait()
    order_rows = jnp.broadcast_to(order[...], (8, RIM))
    match = jnp.where(rows_iota((RIM, RIM)) == jnp.broadcast_to(order[...], (RIM, RIM)), 1.0, 0.0)
    inverse = lax.dot_general(
        lanes_iota((8, RIM)).astype(F32).astype(BF16),
        match.astype(BF16),
        (((1,), (1,)), ((), ())),
        preferred_element_type=F32,
    ).astype(jnp.int32)
    sources = field_rows(source)

    @pl.when(me == 0)
    def _():
        up_in[...] = jnp.zeros((3, 8, RIM), F32)

    @pl.when(me == DOM - 1)
    def _():
        down_in[...] = jnp.zeros((3, 8, RIM), F32)

    def send_rims(k, field):
        down_out[k] = permuted(field[:, :RIM], inverse)
        up_out[k] = field[:, EDGES - RIM :]
        copies = (
            pltpu.make_async_remote_copy(
                src_ref=down_out.at[k],
                dst_ref=down_in.at[k],
                send_sem=down_send.at[k],
                recv_sem=down_recv.at[k],
                device_id=(my_freq, below),
                device_id_type=MESH,
            ),
            pltpu.make_async_remote_copy(
                src_ref=up_out.at[k],
                dst_ref=up_in.at[k],
                send_sem=up_send.at[k],
                recv_sem=up_recv.at[k],
                device_id=(my_freq, above),
                device_id_type=MESH,
            ),
        )
        pl.when(me > 0)(copies[0].start)
        pl.when(me < DOM - 1)(copies[1].start)
        return copies

    def take_rims(k, copies):
        pl.when(me < DOM - 1)(copies[0].wait_recv)
        pl.when(me > 0)(copies[1].wait_recv)
        return permuted(up_in[k], order_rows), down_in[k]

    def join(field, rims):
        low, high = rims
        return jnp.concatenate(
            [field[:, :RIM] + low, field[:, RIM : EDGES - RIM], field[:, EDGES - RIM :] + high], axis=1
        )

    pl.semaphore_wait(barrier, len(NEAR) + 2 + end_pair.astype(jnp.int32) + start_pair.astype(jnp.int32))
    rims0 = send_rims(0, sources)
    for k in ONE_HOP:
        signal(round_two, my_freq, me ^ k)
    for d in (1, 7):
        signal(round_two, lax.rem(my_freq + d, FREQ), me)

    loads[2].wait()

    def tables(q, carry):
        for i in range(6):
            index = halves(edges, i, q)
            ids[q, i] = index
            wide = index >> 7
            for c in range(CHUNKS):
                hit = jnp.where(wide == c, 1.0, 0.0)
                masks[q, c, :, 128 * i : 128 * (i + 1)] = jnp.concatenate([hit] * PARTS, axis=0).astype(BF16)
        for h in range(2):
            at = pl.ds(pl.multiple_of(512 * h + 128 * q, 128), 128)
            stacked = spread(edges[0, :, at])
            for i in range(1, 6):
                stacked = jnp.where(sub == i, spread(edges[i, :, at]), stacked)
            columns = jnp.transpose(stacked & 127)
            for i in range(6):
                hit = jnp.broadcast_to(columns[:, i : i + 1], (128, 128)) == lanes_iota((128, 128))
                onehot[q, 128 * i : 128 * (i + 1), 128 * h : 128 * (h + 1)] = jnp.where(hit, 1.0, 0.0).astype(BF16)
        return carry

    lax.fori_loop(0, GROUPS, tables, 0)

    for n in range(3, 9):
        loads[n].wait()
    omega = jnp.where(sub % 4 < 2, angular[0], angular[1])
    forwards = field_rows(forward)

    def elements(q, carry):
        alive = halves(live, 0, q).astype(F32)
        shift = omega * (halves(conductivity, 0, q) * alive)
        picked = [pick(forwards, ids[q, j]) for j in range(6)]
        for i in range(6):
            running = None
            for j in range(6):
                n = 6 * i + j
                mass_rows = halves(mass, n, q)
                blocks[q, n] = halves(stiffness, n, q) * alive + shift * mass_rows
                product = mass_rows * picked[j]
                running = product if running is None else running + product
            weight[q, i] = omega * running
        return carry

    lax.fori_loop(0, GROUPS, elements, 0)

    pl.semaphore_wait(round_two, len(ONE_HOP) + 2)
    for k in TWO_HOPS:
        signal(round_three, my_freq, me ^ k)
    for d in (2, 6):
        signal(round_three, lax.rem(my_freq + d, FREQ), me)

    def apply(pick_all):
        out = None
        terms_of = []
        for q in range(GROUPS):
            index = [ids[q, i] for i in range(6)]
            picked = [pick_all(index[i]) for i in range(6)]
            term = weight[q, 0] * picked[0]
            for i in range(1, 6):
                term = term + weight[q, i] * picked[i]
            terms_of.append(term)
            columns = []
            for i in range(6):
                running = blocks[q, 6 * i] * picked[0]
                for j in range(1, 6):
                    running = running + blocks[q, 6 * i + j] * picked[j]
                head = running.astype(BF16).astype(F32)
                stacked = jnp.concatenate([head, running - head], axis=0).astype(BF16)
                columns.append(
                    jnp.concatenate(
                        [stacked * masks[q, c, :, 128 * i : 128 * (i + 1)] for c in range(CHUNKS)], axis=0
                    )
                )
            product = lax.dot_general(
                jnp.concatenate(columns, axis=1),
                onehot[q],
                (((1,), (0,)), ((), ())),
                preferred_element_type=F32,
            )
            out = product if out is None else out + product
        pieces = []
        for c in range(CHUNKS):
            both = out[STACK * c : STACK * c + 8] + out[STACK * c + 8 : STACK * c + 16]
            mixed = jnp.where(upper, both[:, :128], both[:, 128:])
            pieces.append(mixed + pltpu.roll(mixed, 4, 0))
        return jnp.concatenate(pieces, axis=1), jnp.concatenate(terms_of, axis=1)

    def apply_own(field):
        return apply(lambda index: pick(field, index))

    def apply_rims(rims):
        low, high = rims
        return apply(lambda index: pick_rims(low, high, index))

    def send_sums(k, quantities):
        row = jnp.zeros((8, 128), F32)
        for n, quantity in enumerate(quantities):
            column = jnp.sum(quantity, axis=1, keepdims=True)
            row = row + jnp.where((lane == 4 * n + sub) & upper, column, 0.0)
        sums[k, me] = jnp.sum(row, axis=0, keepdims=True)
        for n in DOM_PEERS:
            pltpu.make_async_remote_copy(
                src_ref=sums.at[k, me],
                dst_ref=sums.at[k, me],
                send_sem=sum_send.at[k],
                recv_sem=sum_recv.at[k],
                device_id=(my_freq, me ^ n),
                device_id_type=MESH,
            ).start()

    def take_sums(k, count):
        rest = sums.at[k, pl.ds(0, DOM - 1)]
        pltpu.make_async_copy(rest, rest, sum_recv.at[k]).wait()
        total = spread(jnp.sum(sums[k], axis=0))
        return [
            jnp.sum(jnp.where(lane == 4 * n + sub % 4, total, 0.0), axis=1, keepdims=True)
            for n in range(count)
        ]

    own = jnp.where(me > 0, 0.0, 1.0).astype(F32)

    def finish(k, copies, own_part):
        rims = take_rims(k, copies)
        image, term = apply_rims(rims)
        return rims, own_part[0] + image, own_part[1] + term

    part = apply_own(sources)
    rims, image0, term0 = finish(0, rims0, part)
    rims1 = send_rims(1, image0)
    base = join(sources, rims)
    pl.semaphore_wait(round_three, len(TWO_HOPS) + 2)
    send_sums(0, [edge_dot(base, base, own), edge_dot(base, image0)])
    part = apply_own(image0)
    rims, image1, term1 = finish(1, rims1, part)
    rims2 = send_rims(2, image1)
    first = join(image0, rims)
    part = apply_own(image1)

    norm0, curve0 = take_sums(0, 2)
    alpha0 = norm0 / curve0
    residual = base - alpha0 * first
    residual_image = image0 - alpha0 * image1
    early = [
        edge_dot(residual, residual, own),
        edge_dot(residual, residual_image),
        edge_dot(base, residual_image),
        edge_dot(first, first, own),
        edge_dot(first, image1),
    ]
    near = term0 - alpha0 * term1

    rims, image2, term2 = finish(2, rims2, part)
    second = join(image1, rims)
    turned = first - alpha0 * second
    turned_image = image1 - alpha0 * image2
    send_sums(
        1,
        early
        + [
            edge_dot(turned, turned, own),
            edge_dot(first, turned, own),
            edge_dot(turned, turned_image),
            edge_dot(first, turned_image),
        ],
    )
    far = term1 - alpha0 * term2

    norm1, rr1, br1, bb2, bb3, rr2, br2, rr3, br3 = take_sums(1, 9)
    beta0 = norm1 / norm0
    along1 = rr1 + beta0 * br1
    curve1 = along1 + beta0 * (br1 + beta0 * curve0)
    alpha1 = norm1 / curve1
    square = rr2 + beta0 * (2.0 * br2 + beta0 * bb2)
    norm2 = norm1 - alpha1 * (2.0 * along1 - alpha1 * square)
    self2 = rr1 - alpha1 * (2.0 * (rr2 + beta0 * br2) - alpha1 * (rr3 + beta0 * (2.0 * br3 + beta0 * bb3)))
    cross2 = along1 - alpha1 * square
    beta1 = norm2 / norm1
    curve2 = self2 + beta1 * (2.0 * cross2 + beta1 * curve1)
    alpha2 = norm2 / curve2
    on_d1 = alpha1 + alpha2 * beta1
    total = (
        (alpha0 + on_d1 * beta0) * term0
        + (on_d1 + alpha2) * near
        - (alpha2 * alpha1) * (far + beta0 * term1)
    )

    total = total + pltpu.roll(total, 1, 0)
    total = total + pltpu.roll(total, 2, 0)
    packed = jnp.zeros((8, 128), F32)
    for h in range(2):
        for q in range(GROUPS):
            piece = spread(total[4 * h + 3 : 4 * h + 4, 128 * q : 128 * (q + 1)])
            packed = jnp.where(sub == 4 * h + q, piece, packed)
    terms[my_freq] = packed
    for n in FREQ_PEERS:
        peer = lax.rem(my_freq + n, FREQ)
        pltpu.make_async_remote_copy(
            src_ref=terms.at[my_freq],
            dst_ref=terms.at[my_freq],
            send_sem=term_send,
            recv_sem=term_recv,
            device_id=(peer, me),
            device_id_type=MESH,
        ).start()
    for copies in (rims0, rims1, rims2):
        pl.when(me > 0)(copies[0].wait_send)
        pl.when(me < DOM - 1)(copies[1].wait_send)
    for k in range(2):
        sent = sums.at[k, pl.ds(0, DOM - 1)]
        pltpu.make_async_copy(sent, sent, sum_send.at[k]).wait()
    rest = terms.at[pl.ds(0, FREQ - 1)]
    pltpu.make_async_copy(rest, rest, term_recv).wait()
    added = terms[0]
    for n in range(1, FREQ):
        added = added + terms[n]
    for r in range(8):
        total_ref[:, 128 * r : 128 * (r + 1)] = added[r : r + 1]
    pltpu.make_async_copy(rest, rest, term_send).wait()


def local(
    angular,
    stiffness,
    mass_matrix,
    conductivity,
    element_edges,
    live_slots,
    adjoint_source,
    forward_field,
    neighbour_map,
):
    hbm = pl.BlockSpec(memory_space=pltpu.MemorySpace.HBM)
    dma = pltpu.SemaphoreType.DMA
    total = pl.pallas_call(
        kernel,
        out_shape=pltpu.VMEM((1, 1024), F32),
        in_specs=[hbm] * 9,
        out_specs=pl.BlockSpec(memory_space=pltpu.MemorySpace.VMEM),
        scratch_shapes=[
            pltpu.SMEM((2,), F32),
            pltpu.VMEM((36, 1, 1024), F32),
            pltpu.VMEM((36, 1, 1024), F32),
            pltpu.VMEM((1, 1, 1024), F32),
            pltpu.VMEM((6, 1, 1024), jnp.int32),
            pltpu.VMEM((1, 1, 1024), jnp.int32),
            pltpu.VMEM((2, 2, 1, EDGES), F32),
            pltpu.VMEM((2, 2, 1, EDGES), F32),
            pltpu.VMEM((1, RIM), jnp.int32),
            pltpu.VMEM((GROUPS, 6, 8, 128), jnp.int32),
            pltpu.VMEM((GROUPS, CHUNKS, STACK, 768), BF16),
            pltpu.VMEM((GROUPS, 768, 256), BF16),
            pltpu.VMEM((GROUPS, 36, 8, 128), F32),
            pltpu.VMEM((GROUPS, 6, 8, 128), F32),
            pltpu.VMEM((3, 8, RIM), F32),
            pltpu.VMEM((3, 8, RIM), F32),
            pltpu.VMEM((3, 8, RIM), F32),
            pltpu.VMEM((3, 8, RIM), F32),
            pltpu.VMEM((2, DOM, 1, 128), F32),
            pltpu.VMEM((FREQ, 8, 128), F32),
            dma((9,)),
            dma((3,)),
            dma((3,)),
            dma((3,)),
            dma((3,)),
            dma((3,)),
            dma((3,)),
            dma,
            dma,
            pltpu.SemaphoreType.REGULAR,
            pltpu.SemaphoreType.REGULAR,
        ],
        compiler_params=pltpu.CompilerParams(collective_id=0, has_side_effects=True),
    )(
        angular,
        jnp.transpose(stiffness, (1, 0, 2)),
        jnp.transpose(mass_matrix, (1, 0, 2)),
        conductivity[None],
        jnp.transpose(element_edges, (1, 0, 2)),
        live_slots[None],
        adjoint_source,
        forward_field,
        neighbour_map,
    )
    gradient = -total * live_slots.astype(F32)
    updated = conductivity * jnp.exp(-0.5 * jnp.tanh(gradient))
    return gradient, updated


def solution(mesh):
    return jax.shard_map(
        local,
        mesh=mesh,
        in_specs=(
            P("freq"),
            P("dom", None, None),
            P("dom", None, None),
            P("dom", None),
            P("dom", None, None),
            P("dom", None),
            P("freq", None, "dom", None),
            P("freq", None, "dom", None),
            P("dom", None),
        ),
        out_specs=(P("dom", None), P("dom", None)),
        check_vma=False,
    )
```

```python
import jax
import jax.numpy as jnp
from jax import lax
from jax.experimental import pallas as pl
from jax.experimental.pallas import tpu as pltpu
from jax.sharding import PartitionSpec as P

MESH = pl.DeviceIdType.MESH
F32 = jnp.float32
BF16 = jnp.bfloat16
DOM = 32
FREQ = 8
RIM = 256
EDGES = 1280
CHUNKS = EDGES // 128
GROUPS = 4
PARTS = 2
STACK = 8 * PARTS
HOPS = (0, 1, 2, 1)
DOM_PEERS = sorted(range(1, DOM), key=lambda k: (-HOPS[k // 8] - HOPS[k // 2 % 4], k))
FREQ_PEERS = (4, 3, 5, 2, 6, 1, 7)
NEAR = [k for k in range(1, DOM) if HOPS[k // 8] + HOPS[k // 2 % 4] <= 1]
ONE_HOP = [k for k in NEAR if k % 2 == 0]
TWO_HOPS = [k for k in range(0, DOM, 2) if HOPS[k // 8] + HOPS[k // 2 % 4] == 2]


def rows_iota(shape):
    return lax.broadcasted_iota(jnp.int32, shape, 0)


def lanes_iota(shape):
    return lax.broadcasted_iota(jnp.int32, shape, 1)


def lane_pick(table, lane):
    return jnp.take_along_axis(table, lane, axis=1, mode="promise_in_bounds")


def spread(row):
    return jnp.broadcast_to(row, (8, 128))


def chunk(field, c):
    return field[:, 128 * c : 128 * (c + 1)]


def field_rows(ref):
    out = jnp.broadcast_to(ref[0, 0], (8, EDGES))
    kind = rows_iota((8, EDGES)) % 4
    for v in range(1, 4):
        out = jnp.where(kind == v, jnp.broadcast_to(ref[v // 2, v % 2], (8, EDGES)), out)
    return out


def permuted(rim, order):
    out = []
    for q in range(2):
        index = chunk(order, q)
        lane = index & 127
        low = lane_pick(rim[:, :128], lane)
        high = lane_pick(rim[:, 128:], lane)
        out.append(jnp.where(index < 128, low, high))
    return jnp.concatenate(out, axis=1)


def pick(field, index):
    lane = index & 127
    found = [lane_pick(chunk(field, c), lane) for c in range(CHUNKS)]
    bit = 7
    while len(found) > 1:
        odd = (index & (1 << bit)) != 0
        merged = [jnp.where(odd, found[n + 1], found[n]) for n in range(0, len(found) - 1, 2)]
        if len(found) % 2:
            merged.append(found[-1])
        found = merged
        bit += 1
    return found[0]


def pick_rim(rim, index):
    lane = index & 127
    found = jnp.where((index & 128) != 0, lane_pick(rim[:, 128:], lane), lane_pick(rim[:, :128], lane))
    return jnp.where(index < RIM, found, jnp.zeros_like(found))


def edge_dot(a, b, own=None):
    total = chunk(a, 2) * chunk(b, 2)
    for c in range(3, CHUNKS):
        total = total + chunk(a, c) * chunk(b, c)
    rim = chunk(a, 0) * chunk(b, 0) + chunk(a, 1) * chunk(b, 1)
    return total + (rim if own is None else own * rim)


def kernel(
    angular_hbm,
    stiffness_hbm,
    mass_hbm,
    conductivity_hbm,
    edges_hbm,
    live_hbm,
    source_hbm,
    forward_hbm,
    order_hbm,
    total_ref,
    angular,
    stiffness,
    mass,
    conductivity,
    edges,
    live,
    source,
    forward,
    order,
    ids,
    late_ids,
    masks,
    onehot,
    blocks,
    weight,
    down_out,
    up_out,
    rim_in,
    sums,
    terms,
    load_sem,
    down_send,
    up_send,
    rim_recv,
    sum_send,
    sum_recv,
    term_send,
    term_recv,
    round_two,
    round_three,
):
    me = lax.axis_index("dom")
    my_freq = lax.axis_index("freq")
    below = lax.rem(me + DOM - 1, DOM)
    above = lax.rem(me + 1, DOM)

    loads = [
        pltpu.make_async_copy(src, dst, load_sem.at[n])
        for n, (src, dst) in enumerate(
            [
                (source_hbm, source),
                (order_hbm, order),
                (edges_hbm, edges),
                (forward_hbm, forward),
                (stiffness_hbm, stiffness),
                (mass_hbm, mass),
                (conductivity_hbm, conductivity),
                (live_hbm, live),
                (angular_hbm, angular),
            ]
        )
    ]
    for load in loads:
        load.start()

    barrier = pltpu.get_barrier_semaphore()
    row_end = lax.rem(me, 8) == 7
    row_start = lax.rem(me, 8) == 0
    end_pair = row_end & (me < DOM - 1)
    start_pair = row_start & (me > 0)

    def signal(semaphore, freq, dom):
        pl.semaphore_signal(semaphore, inc=1, device_id=(freq, dom), device_id_type=MESH)

    pl.when(end_pair)(lambda: signal(barrier, my_freq, above))
    pl.when(start_pair)(lambda: signal(barrier, my_freq, below))
    for k in NEAR:
        signal(barrier, my_freq, me ^ k)
    for d in (1, 7):
        signal(barrier, lax.rem(my_freq + d, FREQ), me)

    lane = lanes_iota((8, 128))
    sub = rows_iota((8, 128))
    upper = sub < 4

    def halves(ref, n, q):
        first = ref[n, :, pl.ds(pl.multiple_of(128 * q, 128), 128)]
        second = ref[n, :, pl.ds(pl.multiple_of(512 + 128 * q, 128), 128)]
        return jnp.where(upper, spread(first), spread(second))

    loads[0].wait()
    loads[1].wait()
    order_rows = jnp.broadcast_to(order[...], (8, RIM))
    match = jnp.where(rows_iota((RIM, RIM)) == jnp.broadcast_to(order[...], (RIM, RIM)), 1.0, 0.0)
    inverse = lax.dot_general(
        lanes_iota((8, RIM)).astype(F32).astype(BF16),
        match.astype(BF16),
        (((1,), (1,)), ((), ())),
        preferred_element_type=F32,
    ).astype(jnp.int32)
    sources = field_rows(source)

    even = lax.rem(me, 2) == 0
    late_side = lax.rem(me, 2)
    early_side = 1 - late_side
    has_late = (me > 0) & (me < DOM - 1)

    @pl.when(jnp.logical_not(has_late))
    def _():
        for k in range(3):
            rim_in[k, late_side] = jnp.zeros((8, RIM), F32)

    def send_rims(k, field):
        down_out[k] = permuted(field[:, :RIM], inverse)
        up_out[k] = field[:, EDGES - RIM :]
        copies = (
            pltpu.make_async_remote_copy(
                src_ref=down_out.at[k],
                dst_ref=rim_in.at[k, 1],
                send_sem=down_send.at[k],
                recv_sem=rim_recv.at[k, 1],
                device_id=(my_freq, below),
                device_id_type=MESH,
            ),
            pltpu.make_async_remote_copy(
                src_ref=up_out.at[k],
                dst_ref=rim_in.at[k, 0],
                send_sem=up_send.at[k],
                recv_sem=rim_recv.at[k, 0],
                device_id=(my_freq, above),
                device_id_type=MESH,
            ),
        )
        pl.when(me > 0)(copies[0].start)
        pl.when(me < DOM - 1)(copies[1].start)
        return copies

    def take_rim(k, side):
        rim = rim_in.at[k, side]
        return pltpu.make_async_copy(rim, rim, rim_recv.at[k, side]).wait

    def join(field, rim, low_side):
        zero = jnp.zeros((8, RIM), F32)
        return jnp.concatenate(
            [
                field[:, :RIM] + jnp.where(low_side, permuted(rim, order_rows), zero),
                field[:, RIM : EDGES - RIM],
                field[:, EDGES - RIM :] + jnp.where(low_side, zero, rim),
            ],
            axis=1,
        )

    pl.semaphore_wait(barrier, len(NEAR) + 2 + end_pair.astype(jnp.int32) + start_pair.astype(jnp.int32))
    rims0 = send_rims(0, sources)
    for k in ONE_HOP:
        signal(round_two, my_freq, me ^ k)
    for d in (1, 7):
        signal(round_two, lax.rem(my_freq + d, FREQ), me)

    loads[2].wait()

    def tables(q, carry):
        for i in range(6):
            index = halves(edges, i, q)
            ids[q, i] = index
            mapped = pick_rim(order_rows, index)
            late_ids[q, i] = jnp.where(even, jnp.where(index < RIM, mapped, RIM), jnp.where(index >= EDGES - RIM, index - (EDGES - RIM), RIM))
            wide = index >> 7
            for c in range(CHUNKS):
                hit = jnp.where(wide == c, 1.0, 0.0)
                masks[q, c, :, 128 * i : 128 * (i + 1)] = jnp.concatenate([hit] * PARTS, axis=0).astype(BF16)
        for h in range(2):
            at = pl.ds(pl.multiple_of(512 * h + 128 * q, 128), 128)
            stacked = spread(edges[0, :, at])
            for i in range(1, 6):
                stacked = jnp.where(sub == i, spread(edges[i, :, at]), stacked)
            columns = jnp.transpose(stacked & 127)
            for i in range(6):
                hit = jnp.broadcast_to(columns[:, i : i + 1], (128, 128)) == lanes_iota((128, 128))
                onehot[q, 128 * i : 128 * (i + 1), 128 * h : 128 * (h + 1)] = jnp.where(hit, 1.0, 0.0).astype(BF16)
        return carry

    lax.fori_loop(0, GROUPS, tables, 0)

    for n in range(3, 9):
        loads[n].wait()
    omega = jnp.where(sub % 4 < 2, angular[0], angular[1])
    forwards = field_rows(forward)

    def elements(q, carry):
        alive = halves(live, 0, q).astype(F32)
        shift = omega * (halves(conductivity, 0, q) * alive)
        picked = [pick(forwards, ids[q, j]) for j in range(6)]
        for i in range(6):
            running = None
            for j in range(6):
                n = 6 * i + j
                mass_rows = halves(mass, n, q)
                blocks[q, n] = halves(stiffness, n, q) * alive + shift * mass_rows
                product = mass_rows * picked[j]
                running = product if running is None else running + product
            weight[q, i] = omega * running
        return carry

    lax.fori_loop(0, GROUPS, elements, 0)

    pl.semaphore_wait(round_two, len(ONE_HOP) + 2)
    for k in TWO_HOPS:
        signal(round_three, my_freq, me ^ k)
    for d in (2, 6):
        signal(round_three, lax.rem(my_freq + d, FREQ), me)

    def apply(pick_all):
        out = None
        terms_of = []
        for q in range(GROUPS):
            picked = [pick_all(q, i) for i in range(6)]
            term = weight[q, 0] * picked[0]
            for i in range(1, 6):
                term = term + weight[q, i] * picked[i]
            terms_of.append(term)
            columns = []
            for i in range(6):
                running = blocks[q, 6 * i] * picked[0]
                for j in range(1, 6):
                    running = running + blocks[q, 6 * i + j] * picked[j]
                head = running.astype(BF16).astype(F32)
                stacked = jnp.concatenate([head, running - head], axis=0).astype(BF16)
                columns.append(
                    jnp.concatenate(
                        [stacked * masks[q, c, :, 128 * i : 128 * (i + 1)] for c in range(CHUNKS)], axis=0
                    )
                )
            product = lax.dot_general(
                jnp.concatenate(columns, axis=1),
                onehot[q],
                (((1,), (0,)), ((), ())),
                preferred_element_type=F32,
            )
            out = product if out is None else out + product
        pieces = []
        for c in range(CHUNKS):
            both = out[STACK * c : STACK * c + 8] + out[STACK * c + 8 : STACK * c + 16]
            mixed = jnp.where(upper, both[:, :128], both[:, 128:])
            pieces.append(mixed + pltpu.roll(mixed, 4, 0))
        return jnp.concatenate(pieces, axis=1), jnp.concatenate(terms_of, axis=1)

    def apply_early(k, field):
        take_rim(k, early_side)()
        joined = join(field, rim_in[k, early_side], jnp.logical_not(even))
        return joined, apply(lambda q, i: pick(joined, ids[q, i]))

    def apply_late(k, part):
        pl.when(has_late)(take_rim(k, late_side))
        rim = rim_in[k, late_side]
        image, term = apply(lambda q, i: pick_rim(rim, late_ids[q, i]))
        return rim, part[0] + image, part[1] + term

    def pack_sums(start, quantities):
        row = jnp.zeros((8, 128), F32)
        for n, quantity in enumerate(quantities, start):
            column = jnp.sum(quantity, axis=1, keepdims=True)
            row = row + jnp.where((lane == 4 * n + sub) & upper, column, 0.0)
        return jnp.sum(row, axis=0, keepdims=True)

    def send_sums(k, row):
        sums[k, me] = row
        for n in DOM_PEERS:
            pltpu.make_async_remote_copy(
                src_ref=sums.at[k, me],
                dst_ref=sums.at[k, me],
                send_sem=sum_send.at[k],
                recv_sem=sum_recv.at[k],
                device_id=(my_freq, me ^ n),
                device_id_type=MESH,
            ).start()

    def take_sums(k, count):
        rest = sums.at[k, pl.ds(0, DOM - 1)]
        pltpu.make_async_copy(rest, rest, sum_recv.at[k]).wait()
        total = spread(jnp.sum(sums[k], axis=0))
        return [
            jnp.sum(jnp.where(lane == 4 * n + sub % 4, total, 0.0), axis=1, keepdims=True)
            for n in range(count)
        ]

    own = jnp.where(me > 0, 0.0, 1.0).astype(F32)

    base, part = apply_early(0, sources)
    rim, image0, term0 = apply_late(0, part)
    rims1 = send_rims(1, image0)
    base = join(base, rim, even)
    pl.semaphore_wait(round_three, len(TWO_HOPS) + 2)
    send_sums(0, pack_sums(0, [edge_dot(base, base, own), edge_dot(base, image0)]))
    first, part = apply_early(1, image0)
    rim, image1, term1 = apply_late(1, part)
    rims2 = send_rims(2, image1)
    first = join(first, rim, even)
    second, part = apply_early(2, image1)

    norm0, curve0 = take_sums(0, 2)
    alpha0 = norm0 / curve0
    residual = base - alpha0 * first
    residual_image = image0 - alpha0 * image1
    early_sums = pack_sums(
        0,
        [
            edge_dot(residual, residual, own),
            edge_dot(residual, residual_image),
            edge_dot(base, residual_image),
            edge_dot(first, first, own),
            edge_dot(first, image1),
        ],
    )
    near = term0 - alpha0 * term1

    rim, image2, term2 = apply_late(2, part)
    second = join(second, rim, even)
    turned = first - alpha0 * second
    turned_image = image1 - alpha0 * image2
    late_sums = pack_sums(
        5,
        [
            edge_dot(turned, turned, own),
            edge_dot(first, turned, own),
            edge_dot(turned, turned_image),
            edge_dot(first, turned_image),
        ],
    )
    send_sums(1, early_sums + late_sums)
    far = term1 - alpha0 * term2

    norm1, rr1, br1, bb2, bb3, rr2, br2, rr3, br3 = take_sums(1, 9)
    beta0 = norm1 / norm0
    along1 = rr1 + beta0 * br1
    curve1 = along1 + beta0 * (br1 + beta0 * curve0)
    alpha1 = norm1 / curve1
    square = rr2 + beta0 * (2.0 * br2 + beta0 * bb2)
    norm2 = norm1 - alpha1 * (2.0 * along1 - alpha1 * square)
    self2 = rr1 - alpha1 * (2.0 * (rr2 + beta0 * br2) - alpha1 * (rr3 + beta0 * (2.0 * br3 + beta0 * bb3)))
    cross2 = along1 - alpha1 * square
    beta1 = norm2 / norm1
    curve2 = self2 + beta1 * (2.0 * cross2 + beta1 * curve1)
    alpha2 = norm2 / curve2
    on_d1 = alpha1 + alpha2 * beta1
    total = (
        (alpha0 + on_d1 * beta0) * term0
        + (on_d1 + alpha2) * near
        - (alpha2 * alpha1) * (far + beta0 * term1)
    )

    total = total + pltpu.roll(total, 1, 0)
    total = total + pltpu.roll(total, 2, 0)
    packed = jnp.zeros((8, 128), F32)
    for h in range(2):
        for q in range(GROUPS):
            piece = spread(total[4 * h + 3 : 4 * h + 4, 128 * q : 128 * (q + 1)])
            packed = jnp.where(sub == 4 * h + q, piece, packed)
    terms[my_freq] = packed
    for n in FREQ_PEERS:
        peer = lax.rem(my_freq + n, FREQ)
        pltpu.make_async_remote_copy(
            src_ref=terms.at[my_freq],
            dst_ref=terms.at[my_freq],
            send_sem=term_send,
            recv_sem=term_recv,
            device_id=(peer, me),
            device_id_type=MESH,
        ).start()
    for copies in (rims0, rims1, rims2):
        pl.when(me > 0)(copies[0].wait_send)
        pl.when(me < DOM - 1)(copies[1].wait_send)
    for k in range(2):
        sent = sums.at[k, pl.ds(0, DOM - 1)]
        pltpu.make_async_copy(sent, sent, sum_send.at[k]).wait()
    rest = terms.at[pl.ds(0, FREQ - 1)]
    pltpu.make_async_copy(rest, rest, term_recv).wait()
    added = terms[0]
    for n in range(1, FREQ):
        added = added + terms[n]
    for r in range(8):
        total_ref[:, 128 * r : 128 * (r + 1)] = added[r : r + 1]
    pltpu.make_async_copy(rest, rest, term_send).wait()


def local(
    angular,
    stiffness,
    mass_matrix,
    conductivity,
    element_edges,
    live_slots,
    adjoint_source,
    forward_field,
    neighbour_map,
):
    hbm = pl.BlockSpec(memory_space=pltpu.MemorySpace.HBM)
    dma = pltpu.SemaphoreType.DMA
    total = pl.pallas_call(
        kernel,
        out_shape=pltpu.VMEM((1, 1024), F32),
        in_specs=[hbm] * 9,
        out_specs=pl.BlockSpec(memory_space=pltpu.MemorySpace.VMEM),
        scratch_shapes=[
            pltpu.SMEM((2,), F32),
            pltpu.VMEM((36, 1, 1024), F32),
            pltpu.VMEM((36, 1, 1024), F32),
            pltpu.VMEM((1, 1, 1024), F32),
            pltpu.VMEM((6, 1, 1024), jnp.int32),
            pltpu.VMEM((1, 1, 1024), jnp.int32),
            pltpu.VMEM((2, 2, 1, EDGES), F32),
            pltpu.VMEM((2, 2, 1, EDGES), F32),
            pltpu.VMEM((1, RIM), jnp.int32),
            pltpu.VMEM((GROUPS, 6, 8, 128), jnp.int32),
            pltpu.VMEM((GROUPS, 6, 8, 128), jnp.int32),
            pltpu.VMEM((GROUPS, CHUNKS, STACK, 768), BF16),
            pltpu.VMEM((GROUPS, 768, 256), BF16),
            pltpu.VMEM((GROUPS, 36, 8, 128), F32),
            pltpu.VMEM((GROUPS, 6, 8, 128), F32),
            pltpu.VMEM((3, 8, RIM), F32),
            pltpu.VMEM((3, 8, RIM), F32),
            pltpu.VMEM((3, 2, 8, RIM), F32),
            pltpu.VMEM((2, DOM, 1, 128), F32),
            pltpu.VMEM((FREQ, 8, 128), F32),
            dma((9,)),
            dma((3,)),
            dma((3,)),
            dma((3, 2)),
            dma((3,)),
            dma((3,)),
            dma,
            dma,
            pltpu.SemaphoreType.REGULAR,
            pltpu.SemaphoreType.REGULAR,
        ],
        compiler_params=pltpu.CompilerParams(collective_id=0, has_side_effects=True),
    )(
        angular,
        jnp.transpose(stiffness, (1, 0, 2)),
        jnp.transpose(mass_matrix, (1, 0, 2)),
        conductivity[None],
        jnp.transpose(element_edges, (1, 0, 2)),
        live_slots[None],
        adjoint_source,
        forward_field,
        neighbour_map,
    )
    gradient = -total * live_slots.astype(F32)
    updated = conductivity * jnp.exp(-0.5 * jnp.tanh(gradient))
    return gradient, updated


def solution(mesh):
    return jax.shard_map(
        local,
        mesh=mesh,
        in_specs=(
            P("freq"),
            P("dom", None, None),
            P("dom", None, None),
            P("dom", None),
            P("dom", None, None),
            P("dom", None),
            P("freq", None, "dom", None),
            P("freq", None, "dom", None),
            P("dom", None),
        ),
        out_specs=(P("dom", None), P("dom", None)),
        check_vma=False,
    )
```

```python
import jax
import jax.numpy as jnp
from jax import lax
from jax.experimental import pallas as pl
from jax.experimental.pallas import tpu as pltpu
from jax.sharding import PartitionSpec as P

MESH = pl.DeviceIdType.MESH
F32 = jnp.float32
BF16 = jnp.bfloat16
DOM = 32
FREQ = 8
RIM = 256
EDGES = 1280
CHUNKS = EDGES // 128
GROUPS = 4
PARTS = 2
STACK = 8 * PARTS
HOPS = (0, 1, 2, 1)
DOM_PEERS = sorted(range(1, DOM), key=lambda k: (-HOPS[k // 8] - HOPS[k // 2 % 4], k))
FREQ_PEERS = (4, 3, 5, 2, 6, 1, 7)
NEAR = [k for k in range(1, DOM) if HOPS[k // 8] + HOPS[k // 2 % 4] <= 1]
ONE_HOP = [k for k in NEAR if k % 2 == 0]
TWO_HOPS = [k for k in range(0, DOM, 2) if HOPS[k // 8] + HOPS[k // 2 % 4] == 2]


def rows_iota(shape):
    return lax.broadcasted_iota(jnp.int32, shape, 0)


def lanes_iota(shape):
    return lax.broadcasted_iota(jnp.int32, shape, 1)


def lane_pick(table, lane):
    return jnp.take_along_axis(table, lane, axis=1, mode="promise_in_bounds")


def spread(row):
    return jnp.broadcast_to(row, (8, 128))


def chunk(field, c):
    return field[:, 128 * c : 128 * (c + 1)]


def field_rows(ref):
    out = jnp.broadcast_to(ref[0, 0], (8, EDGES))
    kind = rows_iota((8, EDGES)) % 4
    for v in range(1, 4):
        out = jnp.where(kind == v, jnp.broadcast_to(ref[v // 2, v % 2], (8, EDGES)), out)
    return out


def permuted(rim, order):
    out = []
    for q in range(2):
        index = chunk(order, q)
        lane = index & 127
        low = lane_pick(rim[:, :128], lane)
        high = lane_pick(rim[:, 128:], lane)
        out.append(jnp.where(index < 128, low, high))
    return jnp.concatenate(out, axis=1)


def pick(field, index):
    lane = index & 127
    found = [lane_pick(chunk(field, c), lane) for c in range(CHUNKS)]
    bit = 7
    while len(found) > 1:
        odd = (index & (1 << bit)) != 0
        merged = [jnp.where(odd, found[n + 1], found[n]) for n in range(0, len(found) - 1, 2)]
        if len(found) % 2:
            merged.append(found[-1])
        found = merged
        bit += 1
    return found[0]


def pick_rim(rim, index):
    lane = index & 127
    found = jnp.where((index & 128) != 0, lane_pick(rim[:, 128:], lane), lane_pick(rim[:, :128], lane))
    return jnp.where(index < RIM, found, jnp.zeros_like(found))


def edge_dot(a, b, own=None):
    total = chunk(a, 2) * chunk(b, 2)
    for c in range(3, CHUNKS):
        total = total + chunk(a, c) * chunk(b, c)
    rim = chunk(a, 0) * chunk(b, 0) + chunk(a, 1) * chunk(b, 1)
    return total + (rim if own is None else own * rim)


def kernel(
    angular_hbm,
    stiffness_hbm,
    mass_hbm,
    conductivity_hbm,
    edges_hbm,
    live_hbm,
    source_hbm,
    forward_hbm,
    order_hbm,
    total_ref,
    angular,
    stiffness,
    mass,
    conductivity,
    edges,
    live,
    source,
    forward,
    order,
    ids,
    late_ids,
    masks,
    onehot,
    blocks,
    weight,
    kept,
    kept_next,
    down_out,
    up_out,
    rim_in,
    sums,
    terms,
    load_sem,
    down_send,
    up_send,
    rim_recv,
    sum_send,
    sum_recv,
    term_send,
    term_recv,
    round_two,
    round_three,
):
    me = lax.axis_index("dom")
    my_freq = lax.axis_index("freq")
    below = lax.rem(me + DOM - 1, DOM)
    above = lax.rem(me + 1, DOM)

    loads = [
        pltpu.make_async_copy(src, dst, load_sem.at[n])
        for n, (src, dst) in enumerate(
            [
                (source_hbm, source),
                (order_hbm, order),
                (edges_hbm, edges),
                (forward_hbm, forward),
                (stiffness_hbm, stiffness),
                (mass_hbm, mass),
                (conductivity_hbm, conductivity),
                (live_hbm, live),
                (angular_hbm, angular),
            ]
        )
    ]
    for load in loads:
        load.start()

    barrier = pltpu.get_barrier_semaphore()
    row_end = lax.rem(me, 8) == 7
    row_start = lax.rem(me, 8) == 0
    end_pair = row_end & (me < DOM - 1)
    start_pair = row_start & (me > 0)

    def signal(semaphore, freq, dom):
        pl.semaphore_signal(semaphore, inc=1, device_id=(freq, dom), device_id_type=MESH)

    pl.when(end_pair)(lambda: signal(barrier, my_freq, above))
    pl.when(start_pair)(lambda: signal(barrier, my_freq, below))
    for k in NEAR:
        signal(barrier, my_freq, me ^ k)
    for d in (1, 7):
        signal(barrier, lax.rem(my_freq + d, FREQ), me)

    lane = lanes_iota((8, 128))
    sub = rows_iota((8, 128))
    upper = sub < 4

    def halves(ref, n, q):
        first = ref[n, :, pl.ds(pl.multiple_of(128 * q, 128), 128)]
        second = ref[n, :, pl.ds(pl.multiple_of(512 + 128 * q, 128), 128)]
        return jnp.where(upper, spread(first), spread(second))

    loads[0].wait()
    loads[1].wait()
    order_rows = jnp.broadcast_to(order[...], (8, RIM))
    match = jnp.where(rows_iota((RIM, RIM)) == jnp.broadcast_to(order[...], (RIM, RIM)), 1.0, 0.0)
    inverse = lax.dot_general(
        lanes_iota((8, RIM)).astype(F32).astype(BF16),
        match.astype(BF16),
        (((1,), (1,)), ((), ())),
        preferred_element_type=F32,
    ).astype(jnp.int32)
    sources = field_rows(source)

    even = lax.rem(me, 2) == 0
    late_side = lax.rem(me, 2)
    early_side = 1 - late_side
    has_late = (me > 0) & (me < DOM - 1)

    @pl.when(jnp.logical_not(has_late))
    def _():
        for k in range(3):
            rim_in[k, late_side] = jnp.zeros((8, RIM), F32)

    def send_rims(k, field):
        up_out[k] = field[:, EDGES - RIM :]
        copies = (
            pltpu.make_async_remote_copy(
                src_ref=down_out.at[k],
                dst_ref=rim_in.at[k, 1],
                send_sem=down_send.at[k],
                recv_sem=rim_recv.at[k, 1],
                device_id=(my_freq, below),
                device_id_type=MESH,
            ),
            pltpu.make_async_remote_copy(
                src_ref=up_out.at[k],
                dst_ref=rim_in.at[k, 0],
                send_sem=up_send.at[k],
                recv_sem=rim_recv.at[k, 0],
                device_id=(my_freq, above),
                device_id_type=MESH,
            ),
        )
        pl.when(me < DOM - 1)(copies[1].start)
        down_out[k] = permuted(field[:, :RIM], inverse)
        pl.when(me > 0)(copies[0].start)
        return copies

    def take_rim(k, side):
        rim = rim_in.at[k, side]
        return pltpu.make_async_copy(rim, rim, rim_recv.at[k, side]).wait

    def join(field, rim, low_side):
        zero = jnp.zeros((8, RIM), F32)
        return jnp.concatenate(
            [
                field[:, :RIM] + jnp.where(low_side, permuted(rim, order_rows), zero),
                field[:, RIM : EDGES - RIM],
                field[:, EDGES - RIM :] + jnp.where(low_side, zero, rim),
            ],
            axis=1,
        )

    pl.semaphore_wait(barrier, len(NEAR) + 2 + end_pair.astype(jnp.int32) + start_pair.astype(jnp.int32))
    rims0 = send_rims(0, sources)
    for k in ONE_HOP:
        signal(round_two, my_freq, me ^ k)
    for d in (1, 7):
        signal(round_two, lax.rem(my_freq + d, FREQ), me)

    loads[2].wait()

    def tables(q, carry):
        for i in range(6):
            index = halves(edges, i, q)
            ids[q, i] = index
            mapped = pick_rim(order_rows, index)
            late_ids[q, i] = jnp.where(even, jnp.where(index < RIM, mapped, RIM), jnp.where(index >= EDGES - RIM, index - (EDGES - RIM), RIM))
            wide = index >> 7
            for c in range(CHUNKS):
                hit = jnp.where(wide == c, 1.0, 0.0)
                masks[q, c, :, 128 * i : 128 * (i + 1)] = jnp.concatenate([hit] * PARTS, axis=0).astype(BF16)
        for h in range(2):
            at = pl.ds(pl.multiple_of(512 * h + 128 * q, 128), 128)
            stacked = spread(edges[0, :, at])
            for i in range(1, 6):
                stacked = jnp.where(sub == i, spread(edges[i, :, at]), stacked)
            columns = jnp.transpose(stacked & 127)
            for i in range(6):
                hit = jnp.broadcast_to(columns[:, i : i + 1], (128, 128)) == lanes_iota((128, 128))
                onehot[q, 128 * i : 128 * (i + 1), 128 * h : 128 * (h + 1)] = jnp.where(hit, 1.0, 0.0).astype(BF16)
        return carry

    lax.fori_loop(0, GROUPS, tables, 0)

    for n in range(3, 9):
        loads[n].wait()
    omega = jnp.where(sub % 4 < 2, angular[0], angular[1])
    forwards = field_rows(forward)

    def elements(q, carry):
        alive = halves(live, 0, q).astype(F32)
        shift = omega * (halves(conductivity, 0, q) * alive)
        picked = [pick(forwards, ids[q, j]) for j in range(6)]
        for i in range(6):
            running = None
            for j in range(6):
                n = 6 * i + j
                mass_rows = halves(mass, n, q)
                blocks[q, n] = halves(stiffness, n, q) * alive + shift * mass_rows
                product = mass_rows * picked[j]
                running = product if running is None else running + product
            weight[q, i] = omega * running
        return carry

    lax.fori_loop(0, GROUPS, elements, 0)

    pl.semaphore_wait(round_two, len(ONE_HOP) + 2)
    for k in TWO_HOPS:
        signal(round_three, my_freq, me ^ k)
    for d in (2, 6):
        signal(round_three, lax.rem(my_freq + d, FREQ), me)

    def apply(pick_all, keep=None):
        out = None
        terms_of = []
        for q in range(GROUPS):
            picked = [pick_all(q, i) for i in range(6)]
            if keep is not None:
                for i in range(6):
                    kept[q, i] = picked[i] if keep == 0 else kept[q, i] + picked[i]
            term = weight[q, 0] * picked[0]
            for i in range(1, 6):
                term = term + weight[q, i] * picked[i]
            terms_of.append(term)
            columns = []
            for i in range(6):
                running = blocks[q, 6 * i] * picked[0]
                for j in range(1, 6):
                    running = running + blocks[q, 6 * i + j] * picked[j]
                head = running.astype(BF16).astype(F32)
                stacked = jnp.concatenate([head, running - head], axis=0).astype(BF16)
                columns.append(
                    jnp.concatenate(
                        [stacked * masks[q, c, :, 128 * i : 128 * (i + 1)] for c in range(CHUNKS)], axis=0
                    )
                )
            product = lax.dot_general(
                jnp.concatenate(columns, axis=1),
                onehot[q],
                (((1,), (0,)), ((), ())),
                preferred_element_type=F32,
            )
            out = product if out is None else out + product
        pieces = []
        for c in range(CHUNKS):
            both = out[STACK * c : STACK * c + 8] + out[STACK * c + 8 : STACK * c + 16]
            mixed = jnp.where(upper, both[:, :128], both[:, 128:])
            pieces.append(mixed + pltpu.roll(mixed, 4, 0))
        return jnp.concatenate(pieces, axis=1), jnp.concatenate(terms_of, axis=1)

    def join_early(k, field):
        take_rim(k, early_side)()
        return join(field, rim_in[k, early_side], jnp.logical_not(even))

    def late_rim(k):
        pl.when(has_late)(take_rim(k, late_side))
        return rim_in[k, late_side]

    def apply_early(k, field):
        joined = join_early(k, field)
        return joined, apply(lambda q, i: pick(joined, ids[q, i]), keep=0 if k == 1 else None)

    def apply_late(k, part):
        rim = late_rim(k)
        image, term = apply(lambda q, i: pick_rim(rim, late_ids[q, i]), keep=1 if k == 1 else None)
        return rim, part[0] + image, part[1] + term

    def pack_sums(start, quantities):
        row = jnp.zeros((8, 128), F32)
        for n, quantity in enumerate(quantities, start):
            column = jnp.sum(quantity, axis=1, keepdims=True)
            row = row + jnp.where((lane == 4 * n + sub) & upper, column, 0.0)
        return jnp.sum(row, axis=0, keepdims=True)

    def send_sums(k, row):
        sums[k, me] = row
        for n in DOM_PEERS:
            pltpu.make_async_remote_copy(
                src_ref=sums.at[k, me],
                dst_ref=sums.at[k, me],
                send_sem=sum_send.at[k],
                recv_sem=sum_recv.at[k],
                device_id=(my_freq, me ^ n),
                device_id_type=MESH,
            ).start()

    def take_sums(k, count):
        rest = sums.at[k, pl.ds(0, DOM - 1)]
        pltpu.make_async_copy(rest, rest, sum_recv.at[k]).wait()
        total = spread(jnp.sum(sums[k], axis=0))
        return [
            jnp.sum(jnp.where(lane == 4 * n + sub % 4, total, 0.0), axis=1, keepdims=True)
            for n in range(count)
        ]

    own = jnp.where(me > 0, 0.0, 1.0).astype(F32)

    base, part = apply_early(0, sources)
    rim, image0, term0 = apply_late(0, part)
    rims1 = send_rims(1, image0)
    base = join(base, rim, even)
    pl.semaphore_wait(round_three, len(TWO_HOPS) + 2)
    send_sums(0, pack_sums(0, [edge_dot(base, base, own), edge_dot(base, image0)]))
    first, part = apply_early(1, image0)
    rim, image1, term1 = apply_late(1, part)
    rims2 = send_rims(2, image1)
    first = join(first, rim, even)
    second = join_early(2, image1)
    for q in range(GROUPS):
        for i in range(6):
            kept_next[q, i] = pick(second, ids[q, i])

    norm0, curve0 = take_sums(0, 2)
    alpha0 = norm0 / curve0
    residual = base - alpha0 * first
    residual_image = image0 - alpha0 * image1
    early_sums = pack_sums(
        0,
        [
            edge_dot(residual, residual, own),
            edge_dot(residual, residual_image),
            edge_dot(base, residual_image),
            edge_dot(first, first, own),
            edge_dot(first, image1),
        ],
    )
    near = term0 - alpha0 * term1
    for q in range(GROUPS):
        for i in range(6):
            kept[q, i] = kept[q, i] - alpha0 * kept_next[q, i]

    rim = late_rim(2)
    energy = None
    far = []
    for q in range(GROUPS):
        picked = [kept[q, i] - alpha0 * pick_rim(rim, late_ids[q, i]) for i in range(6)]
        term = weight[q, 0] * picked[0]
        for i in range(1, 6):
            term = term + weight[q, i] * picked[i]
        far.append(term)
        for i in range(6):
            running = 0.5 * (blocks[q, 7 * i] * picked[i])
            for j in range(i + 1, 6):
                running = running + blocks[q, 6 * i + j] * picked[j]
            product = picked[i] * running
            energy = product if energy is None else energy + product
    far = jnp.concatenate(far, axis=1)
    energy = 2.0 * (energy + pltpu.roll(energy, 4, 0))
    turned = first - alpha0 * join(second, rim, even)
    late_sums = pack_sums(
        5,
        [
            edge_dot(turned, turned, own),
            edge_dot(first, turned, own),
            energy,
            edge_dot(image1, turned),
        ],
    )
    send_sums(1, early_sums + late_sums)

    norm1, rr1, br1, bb2, bb3, rr2, br2, rr3, br3 = take_sums(1, 9)
    beta0 = norm1 / norm0
    along1 = rr1 + beta0 * br1
    curve1 = along1 + beta0 * (br1 + beta0 * curve0)
    alpha1 = norm1 / curve1
    square = rr2 + beta0 * (2.0 * br2 + beta0 * bb2)
    norm2 = norm1 - alpha1 * (2.0 * along1 - alpha1 * square)
    self2 = rr1 - alpha1 * (2.0 * (rr2 + beta0 * br2) - alpha1 * (rr3 + beta0 * (2.0 * br3 + beta0 * bb3)))
    cross2 = along1 - alpha1 * square
    beta1 = norm2 / norm1
    curve2 = self2 + beta1 * (2.0 * cross2 + beta1 * curve1)
    alpha2 = norm2 / curve2
    on_d1 = alpha1 + alpha2 * beta1
    total = (
        (alpha0 + on_d1 * beta0) * term0
        + (on_d1 + alpha2) * near
        - (alpha2 * alpha1) * (far + beta0 * term1)
    )

    total = total + pltpu.roll(total, 1, 0)
    total = total + pltpu.roll(total, 2, 0)
    packed = jnp.zeros((8, 128), F32)
    for h in range(2):
        for q in range(GROUPS):
            piece = spread(total[4 * h + 3 : 4 * h + 4, 128 * q : 128 * (q + 1)])
            packed = jnp.where(sub == 4 * h + q, piece, packed)
    terms[my_freq] = packed
    for n in FREQ_PEERS:
        peer = lax.rem(my_freq + n, FREQ)
        pltpu.make_async_remote_copy(
            src_ref=terms.at[my_freq],
            dst_ref=terms.at[my_freq],
            send_sem=term_send,
            recv_sem=term_recv,
            device_id=(peer, me),
            device_id_type=MESH,
        ).start()
    for copies in (rims0, rims1, rims2):
        pl.when(me > 0)(copies[0].wait_send)
        pl.when(me < DOM - 1)(copies[1].wait_send)
    for k in range(2):
        sent = sums.at[k, pl.ds(0, DOM - 1)]
        pltpu.make_async_copy(sent, sent, sum_send.at[k]).wait()
    rest = terms.at[pl.ds(0, FREQ - 1)]
    pltpu.make_async_copy(rest, rest, term_recv).wait()
    added = terms[0]
    for n in range(1, FREQ):
        added = added + terms[n]
    for r in range(8):
        total_ref[:, 128 * r : 128 * (r + 1)] = added[r : r + 1]
    pltpu.make_async_copy(rest, rest, term_send).wait()


def local(
    angular,
    stiffness,
    mass_matrix,
    conductivity,
    element_edges,
    live_slots,
    adjoint_source,
    forward_field,
    neighbour_map,
):
    hbm = pl.BlockSpec(memory_space=pltpu.MemorySpace.HBM)
    dma = pltpu.SemaphoreType.DMA
    total = pl.pallas_call(
        kernel,
        out_shape=pltpu.VMEM((1, 1024), F32),
        in_specs=[hbm] * 9,
        out_specs=pl.BlockSpec(memory_space=pltpu.MemorySpace.VMEM),
        scratch_shapes=[
            pltpu.SMEM((2,), F32),
            pltpu.VMEM((36, 1, 1024), F32),
            pltpu.VMEM((36, 1, 1024), F32),
            pltpu.VMEM((1, 1, 1024), F32),
            pltpu.VMEM((6, 1, 1024), jnp.int32),
            pltpu.VMEM((1, 1, 1024), jnp.int32),
            pltpu.VMEM((2, 2, 1, EDGES), F32),
            pltpu.VMEM((2, 2, 1, EDGES), F32),
            pltpu.VMEM((1, RIM), jnp.int32),
            pltpu.VMEM((GROUPS, 6, 8, 128), jnp.int32),
            pltpu.VMEM((GROUPS, 6, 8, 128), jnp.int32),
            pltpu.VMEM((GROUPS, CHUNKS, STACK, 768), BF16),
            pltpu.VMEM((GROUPS, 768, 256), BF16),
            pltpu.VMEM((GROUPS, 36, 8, 128), F32),
            pltpu.VMEM((GROUPS, 6, 8, 128), F32),
            pltpu.VMEM((GROUPS, 6, 8, 128), F32),
            pltpu.VMEM((GROUPS, 6, 8, 128), F32),
            pltpu.VMEM((3, 8, RIM), F32),
            pltpu.VMEM((3, 8, RIM), F32),
            pltpu.VMEM((3, 2, 8, RIM), F32),
            pltpu.VMEM((2, DOM, 1, 128), F32),
            pltpu.VMEM((FREQ, 8, 128), F32),
            dma((9,)),
            dma((3,)),
            dma((3,)),
            dma((3, 2)),
            dma((3,)),
            dma((3,)),
            dma,
            dma,
            pltpu.SemaphoreType.REGULAR,
            pltpu.SemaphoreType.REGULAR,
        ],
        compiler_params=pltpu.CompilerParams(collective_id=0, has_side_effects=True),
    )(
        angular,
        jnp.transpose(stiffness, (1, 0, 2)),
        jnp.transpose(mass_matrix, (1, 0, 2)),
        conductivity[None],
        jnp.transpose(element_edges, (1, 0, 2)),
        live_slots[None],
        adjoint_source,
        forward_field,
        neighbour_map,
    )
    gradient = -total * live_slots.astype(F32)
    updated = conductivity * jnp.exp(-0.5 * jnp.tanh(gradient))
    return gradient, updated


def solution(mesh):
    return jax.shard_map(
        local,
        mesh=mesh,
        in_specs=(
            P("freq"),
            P("dom", None, None),
            P("dom", None, None),
            P("dom", None),
            P("dom", None, None),
            P("dom", None),
            P("freq", None, "dom", None),
            P("freq", None, "dom", None),
            P("dom", None),
        ),
        out_specs=(P("dom", None), P("dom", None)),
        check_vma=False,
    )
```

```python
import jax
import jax.numpy as jnp
from jax import lax
from jax.experimental import pallas as pl
from jax.experimental.pallas import tpu as pltpu
from jax.sharding import PartitionSpec as P

MESH = pl.DeviceIdType.MESH
F32 = jnp.float32
BF16 = jnp.bfloat16
DOM = 32
FREQ = 8
RIM = 256
EDGES = 1280
CHUNKS = EDGES // 128
GROUPS = 4
AHEAD = 2
PARTS = 2
STACK = 8 * PARTS
HOPS = (0, 1, 2, 1)
DOM_PEERS = sorted(range(1, DOM), key=lambda k: (-HOPS[k // 8] - HOPS[k // 2 % 4], k))
FREQ_PEERS = (4, 3, 5, 2, 6, 1, 7)
NEAR = [k for k in range(1, DOM) if HOPS[k // 8] + HOPS[k // 2 % 4] <= 1]
ONE_HOP = [k for k in NEAR if k % 2 == 0]
TWO_HOPS = [k for k in range(0, DOM, 2) if HOPS[k // 8] + HOPS[k // 2 % 4] == 2]


def rows_iota(shape):
    return lax.broadcasted_iota(jnp.int32, shape, 0)


def lanes_iota(shape):
    return lax.broadcasted_iota(jnp.int32, shape, 1)


def lane_pick(table, lane):
    return jnp.take_along_axis(table, lane, axis=1, mode="promise_in_bounds")


def spread(row):
    return jnp.broadcast_to(row, (8, 128))


def chunk(field, c):
    return field[:, 128 * c : 128 * (c + 1)]


def field_rows(ref):
    out = jnp.broadcast_to(ref[0, 0], (8, EDGES))
    kind = rows_iota((8, EDGES)) % 4
    for v in range(1, 4):
        out = jnp.where(kind == v, jnp.broadcast_to(ref[v // 2, v % 2], (8, EDGES)), out)
    return out


def permuted(rim, order):
    out = []
    for q in range(2):
        index = chunk(order, q)
        lane = index & 127
        low = lane_pick(rim[:, :128], lane)
        high = lane_pick(rim[:, 128:], lane)
        out.append(jnp.where(index < 128, low, high))
    return jnp.concatenate(out, axis=1)


def pick(field, index):
    lane = index & 127
    found = [lane_pick(chunk(field, c), lane) for c in range(CHUNKS)]
    bit = 7
    while len(found) > 1:
        odd = (index & (1 << bit)) != 0
        merged = [jnp.where(odd, found[n + 1], found[n]) for n in range(0, len(found) - 1, 2)]
        if len(found) % 2:
            merged.append(found[-1])
        found = merged
        bit += 1
    return found[0]


def pick_rim(rim, index):
    lane = index & 127
    found = jnp.where((index & 128) != 0, lane_pick(rim[:, 128:], lane), lane_pick(rim[:, :128], lane))
    return jnp.where(index < RIM, found, jnp.zeros_like(found))


def edge_dot(a, b, own=None):
    total = chunk(a, 2) * chunk(b, 2)
    for c in range(3, CHUNKS):
        total = total + chunk(a, c) * chunk(b, c)
    rim = chunk(a, 0) * chunk(b, 0) + chunk(a, 1) * chunk(b, 1)
    return total + (rim if own is None else own * rim)


def kernel(
    angular_hbm,
    stiffness_hbm,
    mass_hbm,
    conductivity_hbm,
    edges_hbm,
    live_hbm,
    source_hbm,
    forward_hbm,
    order_hbm,
    total_ref,
    angular,
    stiffness,
    mass,
    conductivity,
    edges,
    live,
    source,
    forward,
    order,
    ids,
    late_ids,
    masks,
    onehot,
    late_masks,
    late_hot,
    blocks,
    weight,
    kept,
    kept_next,
    rim_out,
    rim_in,
    sums,
    terms,
    load_sem,
    rim_send,
    rim_recv,
    sum_send,
    sum_recv,
    term_send,
    term_recv,
    round_two,
    round_three,
):
    me = lax.axis_index("dom")
    my_freq = lax.axis_index("freq")
    below = lax.rem(me + DOM - 1, DOM)
    above = lax.rem(me + 1, DOM)

    loads = [
        pltpu.make_async_copy(src, dst, load_sem.at[n])
        for n, (src, dst) in enumerate(
            [
                (source_hbm, source),
                (order_hbm, order),
                (edges_hbm, edges),
                (forward_hbm, forward),
                (stiffness_hbm, stiffness),
                (mass_hbm, mass),
                (conductivity_hbm, conductivity),
                (live_hbm, live),
                (angular_hbm, angular),
            ]
        )
    ]
    for load in loads:
        load.start()

    barrier = pltpu.get_barrier_semaphore()
    row_end = lax.rem(me, 8) == 7
    row_start = lax.rem(me, 8) == 0
    end_pair = row_end & (me < DOM - 1)
    start_pair = row_start & (me > 0)

    def signal(semaphore, freq, dom):
        pl.semaphore_signal(semaphore, inc=1, device_id=(freq, dom), device_id_type=MESH)

    pl.when(end_pair)(lambda: signal(barrier, my_freq, above))
    pl.when(start_pair)(lambda: signal(barrier, my_freq, below))
    for k in NEAR:
        signal(barrier, my_freq, me ^ k)
    for d in (1, 7):
        signal(barrier, lax.rem(my_freq + d, FREQ), me)

    lane = lanes_iota((8, 128))
    sub = rows_iota((8, 128))
    upper = sub < 4

    def halves(ref, n, q):
        first = ref[n, :, pl.ds(pl.multiple_of(128 * q, 128), 128)]
        second = ref[n, :, pl.ds(pl.multiple_of(512 + 128 * q, 128), 128)]
        return jnp.where(upper, spread(first), spread(second))

    loads[0].wait()
    loads[1].wait()
    order_rows = jnp.broadcast_to(order[...], (8, RIM))
    match = jnp.where(rows_iota((RIM, RIM)) == jnp.broadcast_to(order[...], (RIM, RIM)), 1.0, 0.0)
    inverse = lax.dot_general(
        lanes_iota((8, RIM)).astype(F32).astype(BF16),
        match.astype(BF16),
        (((1,), (1,)), ((), ())),
        preferred_element_type=F32,
    ).astype(jnp.int32)
    sources = field_rows(source)

    even = lax.rem(me, 2) == 0
    late_side = lax.rem(me, 2)
    early_side = 1 - late_side
    has_late = (me > 0) & (me < DOM - 1)

    @pl.when(jnp.logical_not(has_late))
    def _():
        for k in range(3):
            rim_in[k, late_side] = jnp.zeros((8, RIM), F32)

    late_peer = jnp.where(even, below, above)

    def rim_copy(k, n):
        side, peer = ((early_side, late_peer), (late_side, me ^ 1))[n]
        return pltpu.make_async_remote_copy(
            src_ref=rim_out.at[k, n, pl.ds(0, 4)],
            dst_ref=rim_in.at[k, side, pl.ds(0, 4)],
            send_sem=rim_send.at[k, n],
            recv_sem=rim_recv.at[k, side],
            device_id=(my_freq, peer),
            device_id_type=MESH,
        )

    def send_late(k, rim):
        rim_out[k, 0] = jnp.where(even, permuted(rim, inverse), rim)
        pl.when(has_late)(rim_copy(k, 0).start)

    def send_early(k, rim):
        rim_out[k, 1] = jnp.where(even, rim, permuted(rim, inverse))
        rim_copy(k, 1).start()

    def late_part(field):
        return jnp.where(even, field[:, :RIM], field[:, EDGES - RIM :])

    def early_part(field):
        return jnp.where(even, field[:, EDGES - RIM :], field[:, :RIM])

    def take_rim(k, side):
        rim = rim_in.at[k, side, pl.ds(0, 4)]
        return pltpu.make_async_copy(rim, rim, rim_recv.at[k, side]).wait

    def received(k, side):
        rim = rim_in[k, side, pl.ds(0, 4)]
        return jnp.concatenate([rim, rim], axis=0)

    def join(field, rim, low_side):
        zero = jnp.zeros((8, RIM), F32)
        return jnp.concatenate(
            [
                field[:, :RIM] + jnp.where(low_side, permuted(rim, order_rows), zero),
                field[:, RIM : EDGES - RIM],
                field[:, EDGES - RIM :] + jnp.where(low_side, zero, rim),
            ],
            axis=1,
        )

    loads[2].wait()

    def tables(q, carry):
        for i in range(6):
            index = halves(edges, i, q)
            ids[q, i] = index
            mapped = pick_rim(order_rows, index)
            in_late = jnp.where(even, index, index - (EDGES - RIM))
            quarter = jnp.where((in_late >= 0) & (in_late < RIM), in_late >> 6, 4)
            for c in range(4):
                hit = jnp.where(quarter == c, 1.0, 0.0)
                late_masks[q, c, :, 128 * i : 128 * (i + 1)] = jnp.concatenate([hit] * PARTS, axis=0).astype(BF16)
            late_ids[q, i] = jnp.where(even, jnp.where(index < RIM, mapped, RIM), jnp.where(index >= EDGES - RIM, index - (EDGES - RIM), RIM))
            wide = index >> 7
            for c in range(CHUNKS):
                hit = jnp.where(wide == c, 1.0, 0.0)
                masks[q, c, :, 128 * i : 128 * (i + 1)] = jnp.concatenate([hit] * PARTS, axis=0).astype(BF16)
        columns = []
        for h in range(2):
            at = pl.ds(pl.multiple_of(512 * h + 128 * q, 128), 128)
            stacked = spread(edges[0, :, at])
            for i in range(1, 6):
                stacked = jnp.where(sub == i, spread(edges[i, :, at]), stacked)
            columns.append(jnp.transpose(stacked & 127))
        across = lanes_iota((128, 128))
        for i in range(6):
            wide = [jnp.broadcast_to(columns[h][:, i : i + 1], (128, 128)) for h in range(2)]
            for h in range(2):
                onehot[q, 128 * i : 128 * (i + 1), 128 * h : 128 * (h + 1)] = jnp.where(
                    wide[h] == across, 1.0, 0.0
                ).astype(BF16)
            short = jnp.where(across < 64, wide[0] & 63, (wide[1] & 63) + 64)
            late_hot[q, 128 * i : 128 * (i + 1)] = jnp.where(short == across, 1.0, 0.0).astype(BF16)
        return carry

    lax.fori_loop(0, AHEAD, tables, 0)

    pl.semaphore_wait(barrier, len(NEAR) + 2 + end_pair.astype(jnp.int32) + start_pair.astype(jnp.int32))
    send_late(0, late_part(sources))
    send_early(0, early_part(sources))
    for k in ONE_HOP:
        signal(round_two, my_freq, me ^ k)
    for d in (1, 7):
        signal(round_two, lax.rem(my_freq + d, FREQ), me)

    lax.fori_loop(AHEAD, GROUPS, tables, 0)

    for n in range(3, 9):
        loads[n].wait()
    omega = jnp.where(sub % 4 < 2, angular[0], angular[1])
    forwards = field_rows(forward)

    def elements(q, carry):
        alive = halves(live, 0, q).astype(F32)
        shift = omega * (halves(conductivity, 0, q) * alive)
        picked = [pick(forwards, ids[q, j]) for j in range(6)]
        for i in range(6):
            running = None
            for j in range(6):
                n = 6 * i + j
                mass_rows = halves(mass, n, q)
                blocks[q, n] = halves(stiffness, n, q) * alive + shift * mass_rows
                product = mass_rows * picked[j]
                running = product if running is None else running + product
            weight[q, i] = omega * running
        return carry

    lax.fori_loop(0, GROUPS, elements, 0)

    pl.semaphore_wait(round_two, len(ONE_HOP) + 2)
    for k in TWO_HOPS:
        signal(round_three, my_freq, me ^ k)
    for d in (2, 6):
        signal(round_three, lax.rem(my_freq + d, FREQ), me)

    def element_values(pick_all, keep=None):
        terms_of = []
        values = []
        for q in range(GROUPS):
            picked = [pick_all(q, i) for i in range(6)]
            if keep is not None:
                for i in range(6):
                    kept[q, i] = picked[i] if keep == 0 else kept[q, i] + picked[i]
            term = weight[q, 0] * picked[0]
            for i in range(1, 6):
                term = term + weight[q, i] * picked[i]
            terms_of.append(term)
            for i in range(6):
                running = blocks[q, 6 * i] * picked[0]
                for j in range(1, 6):
                    running = running + blocks[q, 6 * i + j] * picked[j]
                head = running.astype(BF16).astype(F32)
                values.append(jnp.concatenate([head, running - head], axis=0).astype(BF16))
        return values, jnp.concatenate(terms_of, axis=1)

    def add_up(values, chosen, table, count):
        out = None
        for q in range(GROUPS):
            columns = [
                jnp.concatenate(
                    [values[6 * q + i] * chosen[q, c, :, 128 * i : 128 * (i + 1)] for c in range(count)], axis=0
                )
                for i in range(6)
            ]
            product = lax.dot_general(
                jnp.concatenate(columns, axis=1), table[q], (((1,), (0,)), ((), ())), preferred_element_type=F32
            )
            out = product if out is None else out + product
        return [out[STACK * c : STACK * c + 8] + out[STACK * c + 8 : STACK * c + 16] for c in range(count)]

    def scatter(values):
        pieces = []
        for both in add_up(values, masks, onehot, CHUNKS):
            mixed = jnp.where(upper, both[:, :128], both[:, 128:])
            pieces.append(mixed + pltpu.roll(mixed, 4, 0))
        return jnp.concatenate(pieces, axis=1)

    def scatter_late(values):
        found = add_up(values, late_masks, late_hot, 4)
        turned_lanes = [pltpu.roll(both, 64, 1) for both in found]
        pieces = []
        for c in (0, 2):
            left = jnp.where(upper, found[c], turned_lanes[c])
            right = jnp.where(upper, turned_lanes[c + 1], found[c + 1])
            mixed = jnp.where(lane < 64, left, right)
            pieces.append(mixed + pltpu.roll(mixed, 4, 0))
        return jnp.concatenate(pieces, axis=1)

    def join_early(k, field):
        take_rim(k, early_side)()
        return join(field, received(k, early_side), jnp.logical_not(even))

    def late_rim(k):
        pl.when(has_late)(take_rim(k, late_side))
        return received(k, late_side)

    def apply_early(k, field):
        joined = join_early(k, field)
        values, term = element_values(lambda q, i: pick(joined, ids[q, i]), keep=0 if k == 1 else None)
        return joined, (scatter(values), term)

    def apply_late(k, part):
        rim = late_rim(k)
        values, term = element_values(lambda q, i: pick_rim(rim, late_ids[q, i]), keep=1 if k == 1 else None)
        send_late(k + 1, late_part(part[0]) + scatter_late(values))
        image = part[0] + scatter(values)
        send_early(k + 1, early_part(image))
        return rim, image, part[1] + term

    def pack_sums(start, quantities):
        row = jnp.zeros((8, 128), F32)
        for n, quantity in enumerate(quantities, start):
            column = jnp.sum(quantity, axis=1, keepdims=True)
            row = row + jnp.where((lane == 4 * n + sub) & upper, column, 0.0)
        return jnp.sum(row, axis=0, keepdims=True)

    def send_sums(k, row):
        sums[k, me] = row
        for n in DOM_PEERS:
            pltpu.make_async_remote_copy(
                src_ref=sums.at[k, me],
                dst_ref=sums.at[k, me],
                send_sem=sum_send.at[k],
                recv_sem=sum_recv.at[k],
                device_id=(my_freq, me ^ n),
                device_id_type=MESH,
            ).start()

    def take_sums(k, count):
        rest = sums.at[k, pl.ds(0, DOM - 1)]
        pltpu.make_async_copy(rest, rest, sum_recv.at[k]).wait()
        total = spread(jnp.sum(sums[k], axis=0))
        return [
            jnp.sum(jnp.where(lane == 4 * n + sub % 4, total, 0.0), axis=1, keepdims=True)
            for n in range(count)
        ]

    own = jnp.where(me > 0, 0.0, 1.0).astype(F32)

    base, part = apply_early(0, sources)
    rim, image0, term0 = apply_late(0, part)
    base = join(base, rim, even)
    pl.semaphore_wait(round_three, len(TWO_HOPS) + 2)
    send_sums(0, pack_sums(0, [edge_dot(base, base, own), edge_dot(base, image0)]))
    first, part = apply_early(1, image0)
    rim, image1, term1 = apply_late(1, part)
    first = join(first, rim, even)
    second = join_early(2, image1)
    for q in range(GROUPS):
        for i in range(6):
            kept_next[q, i] = pick(second, ids[q, i])

    norm0, curve0 = take_sums(0, 2)
    alpha0 = norm0 / curve0
    residual = base - alpha0 * first
    residual_image = image0 - alpha0 * image1
    early_sums = pack_sums(
        0,
        [
            edge_dot(residual, residual, own),
            edge_dot(residual, residual_image),
            edge_dot(base, residual_image),
            edge_dot(first, first, own),
            edge_dot(first, image1),
        ],
    )
    near = term0 - alpha0 * term1
    for q in range(GROUPS):
        for i in range(6):
            kept[q, i] = kept[q, i] - alpha0 * kept_next[q, i]

    rim = late_rim(2)
    energy = None
    far = []
    for q in range(GROUPS):
        picked = [kept[q, i] - alpha0 * pick_rim(rim, late_ids[q, i]) for i in range(6)]
        term = weight[q, 0] * picked[0]
        for i in range(1, 6):
            term = term + weight[q, i] * picked[i]
        far.append(term)
        for i in range(6):
            running = 0.5 * (blocks[q, 7 * i] * picked[i])
            for j in range(i + 1, 6):
                running = running + blocks[q, 6 * i + j] * picked[j]
            product = picked[i] * running
            energy = product if energy is None else energy + product
    far = jnp.concatenate(far, axis=1)
    energy = 2.0 * (energy + pltpu.roll(energy, 4, 0))
    turned = first - alpha0 * join(second, rim, even)
    late_sums = pack_sums(
        5,
        [
            edge_dot(turned, turned, own),
            edge_dot(first, turned, own),
            energy,
            edge_dot(image1, turned),
        ],
    )
    send_sums(1, early_sums + late_sums)

    norm1, rr1, br1, bb2, bb3, rr2, br2, rr3, br3 = take_sums(1, 9)
    beta0 = norm1 / norm0
    along1 = rr1 + beta0 * br1
    curve1 = along1 + beta0 * (br1 + beta0 * curve0)
    alpha1 = norm1 / curve1
    square = rr2 + beta0 * (2.0 * br2 + beta0 * bb2)
    norm2 = norm1 - alpha1 * (2.0 * along1 - alpha1 * square)
    self2 = rr1 - alpha1 * (2.0 * (rr2 + beta0 * br2) - alpha1 * (rr3 + beta0 * (2.0 * br3 + beta0 * bb3)))
    cross2 = along1 - alpha1 * square
    beta1 = norm2 / norm1
    curve2 = self2 + beta1 * (2.0 * cross2 + beta1 * curve1)
    alpha2 = norm2 / curve2
    on_d1 = alpha1 + alpha2 * beta1
    total = (
        (alpha0 + on_d1 * beta0) * term0
        + (on_d1 + alpha2) * near
        - (alpha2 * alpha1) * (far + beta0 * term1)
    )

    total = total + pltpu.roll(total, 1, 0)
    total = total + pltpu.roll(total, 2, 0)
    packed = jnp.zeros((8, 128), F32)
    for h in range(2):
        for q in range(GROUPS):
            piece = spread(total[4 * h + 3 : 4 * h + 4, 128 * q : 128 * (q + 1)])
            packed = jnp.where(sub == 4 * h + q, piece, packed)
    terms[my_freq] = packed
    for n in FREQ_PEERS:
        peer = lax.rem(my_freq + n, FREQ)
        pltpu.make_async_remote_copy(
            src_ref=terms.at[my_freq],
            dst_ref=terms.at[my_freq],
            send_sem=term_send,
            recv_sem=term_recv,
            device_id=(peer, me),
            device_id_type=MESH,
        ).start()
    for k in range(3):
        pl.when(has_late)(rim_copy(k, 0).wait_send)
        rim_copy(k, 1).wait_send()
    for k in range(2):
        sent = sums.at[k, pl.ds(0, DOM - 1)]
        pltpu.make_async_copy(sent, sent, sum_send.at[k]).wait()
    rest = terms.at[pl.ds(0, FREQ - 1)]
    pltpu.make_async_copy(rest, rest, term_recv).wait()
    added = terms[0]
    for n in range(1, FREQ):
        added = added + terms[n]
    for r in range(8):
        total_ref[:, 128 * r : 128 * (r + 1)] = added[r : r + 1]
    pltpu.make_async_copy(rest, rest, term_send).wait()


def local(
    angular,
    stiffness,
    mass_matrix,
    conductivity,
    element_edges,
    live_slots,
    adjoint_source,
    forward_field,
    neighbour_map,
):
    hbm = pl.BlockSpec(memory_space=pltpu.MemorySpace.HBM)
    dma = pltpu.SemaphoreType.DMA
    total = pl.pallas_call(
        kernel,
        out_shape=pltpu.VMEM((1, 1024), F32),
        in_specs=[hbm] * 9,
        out_specs=pl.BlockSpec(memory_space=pltpu.MemorySpace.VMEM),
        scratch_shapes=[
            pltpu.SMEM((2,), F32),
            pltpu.VMEM((36, 1, 1024), F32),
            pltpu.VMEM((36, 1, 1024), F32),
            pltpu.VMEM((1, 1, 1024), F32),
            pltpu.VMEM((6, 1, 1024), jnp.int32),
            pltpu.VMEM((1, 1, 1024), jnp.int32),
            pltpu.VMEM((2, 2, 1, EDGES), F32),
            pltpu.VMEM((2, 2, 1, EDGES), F32),
            pltpu.VMEM((1, RIM), jnp.int32),
            pltpu.VMEM((GROUPS, 6, 8, 128), jnp.int32),
            pltpu.VMEM((GROUPS, 6, 8, 128), jnp.int32),
            pltpu.VMEM((GROUPS, CHUNKS, STACK, 768), BF16),
            pltpu.VMEM((GROUPS, 768, 256), BF16),
            pltpu.VMEM((GROUPS, 4, STACK, 768), BF16),
            pltpu.VMEM((GROUPS, 768, 128), BF16),
            pltpu.VMEM((GROUPS, 36, 8, 128), F32),
            pltpu.VMEM((GROUPS, 6, 8, 128), F32),
            pltpu.VMEM((GROUPS, 6, 8, 128), F32),
            pltpu.VMEM((GROUPS, 6, 8, 128), F32),
            pltpu.VMEM((3, 2, 8, RIM), F32),
            pltpu.VMEM((3, 2, 8, RIM), F32),
            pltpu.VMEM((2, DOM, 1, 128), F32),
            pltpu.VMEM((FREQ, 8, 128), F32),
            dma((9,)),
            dma((3, 2)),
            dma((3, 2)),
            dma((3,)),
            dma((3,)),
            dma,
            dma,
            pltpu.SemaphoreType.REGULAR,
            pltpu.SemaphoreType.REGULAR,
        ],
        compiler_params=pltpu.CompilerParams(collective_id=0, has_side_effects=True),
    )(
        angular,
        jnp.transpose(stiffness, (1, 0, 2)),
        jnp.transpose(mass_matrix, (1, 0, 2)),
        conductivity[None],
        jnp.transpose(element_edges, (1, 0, 2)),
        live_slots[None],
        adjoint_source,
        forward_field,
        neighbour_map,
    )
    gradient = -total * live_slots.astype(F32)
    updated = conductivity * jnp.exp(-0.5 * jnp.tanh(gradient))
    return gradient, updated


def solution(mesh):
    return jax.shard_map(
        local,
        mesh=mesh,
        in_specs=(
            P("freq"),
            P("dom", None, None),
            P("dom", None, None),
            P("dom", None),
            P("dom", None, None),
            P("dom", None),
            P("freq", None, "dom", None),
            P("freq", None, "dom", None),
            P("dom", None),
        ),
        out_specs=(P("dom", None), P("dom", None)),
        check_vma=False,
    )
```

```python
import jax
import jax.numpy as jnp
from jax import lax
from jax.experimental import pallas as pl
from jax.experimental.pallas import tpu as pltpu
from jax.sharding import PartitionSpec as P

MESH = pl.DeviceIdType.MESH
F32 = jnp.float32
BF16 = jnp.bfloat16
DOM = 32
FREQ = 8
RIM = 256
EDGES = 1280
CHUNKS = EDGES // 128
GROUPS = 4
AHEAD = 3
PARTS = 2
STACK = 8 * PARTS
HOPS = (0, 1, 2, 1)
DOM_PEERS = sorted(range(1, DOM), key=lambda k: (-HOPS[k // 8] - HOPS[k // 2 % 4], k))
FREQ_PEERS = (4, 3, 5, 2, 6, 1, 7)
NEAR = [k for k in range(1, DOM) if HOPS[k // 8] + HOPS[k // 2 % 4] <= 1]
ONE_HOP = [k for k in NEAR if k % 2 == 0]
TWO_HOPS = [k for k in range(0, DOM, 2) if HOPS[k // 8] + HOPS[k // 2 % 4] == 2]


def rows_iota(shape):
    return lax.broadcasted_iota(jnp.int32, shape, 0)


def lanes_iota(shape):
    return lax.broadcasted_iota(jnp.int32, shape, 1)


def lane_pick(table, lane):
    return jnp.take_along_axis(table, lane, axis=1, mode="promise_in_bounds")


def spread(row):
    return jnp.broadcast_to(row, (8, 128))


def chunk(field, c):
    return field[:, 128 * c : 128 * (c + 1)]


def field_rows(ref):
    out = jnp.broadcast_to(ref[0, 0], (8, EDGES))
    kind = rows_iota((8, EDGES)) % 4
    for v in range(1, 4):
        out = jnp.where(kind == v, jnp.broadcast_to(ref[v // 2, v % 2], (8, EDGES)), out)
    return out


def permuted(rim, order):
    out = []
    for q in range(2):
        index = chunk(order, q)
        lane = index & 127
        low = lane_pick(rim[:, :128], lane)
        high = lane_pick(rim[:, 128:], lane)
        out.append(jnp.where(index < 128, low, high))
    return jnp.concatenate(out, axis=1)


def pick(field, index):
    lane = index & 127
    found = [lane_pick(chunk(field, c), lane) for c in range(CHUNKS)]
    bit = 7
    while len(found) > 1:
        odd = (index & (1 << bit)) != 0
        merged = [jnp.where(odd, found[n + 1], found[n]) for n in range(0, len(found) - 1, 2)]
        if len(found) % 2:
            merged.append(found[-1])
        found = merged
        bit += 1
    return found[0]


def pick_rim(rim, index):
    lane = index & 127
    found = jnp.where((index & 128) != 0, lane_pick(rim[:, 128:], lane), lane_pick(rim[:, :128], lane))
    return jnp.where(index < RIM, found, jnp.zeros_like(found))


def edge_dot(a, b, own=None):
    total = chunk(a, 2) * chunk(b, 2)
    for c in range(3, CHUNKS):
        total = total + chunk(a, c) * chunk(b, c)
    rim = chunk(a, 0) * chunk(b, 0) + chunk(a, 1) * chunk(b, 1)
    return total + (rim if own is None else own * rim)


def kernel(
    angular_hbm,
    stiffness_hbm,
    mass_hbm,
    conductivity_hbm,
    edges_hbm,
    live_hbm,
    source_hbm,
    forward_hbm,
    order_hbm,
    total_ref,
    angular,
    stiffness,
    mass,
    conductivity,
    edges,
    live,
    source,
    forward,
    order,
    ids,
    late_ids,
    masks,
    onehot,
    late_masks,
    late_hot,
    blocks,
    weight,
    kept,
    kept_next,
    rim_out,
    rim_in,
    sums,
    terms,
    load_sem,
    rim_send,
    rim_recv,
    sum_send,
    sum_recv,
    term_send,
    term_recv,
    round_two,
    round_three,
):
    me = lax.axis_index("dom")
    my_freq = lax.axis_index("freq")
    below = lax.rem(me + DOM - 1, DOM)
    above = lax.rem(me + 1, DOM)

    loads = [
        pltpu.make_async_copy(src, dst, load_sem.at[n])
        for n, (src, dst) in enumerate(
            [
                (source_hbm, source),
                (order_hbm, order),
                (edges_hbm, edges),
                (forward_hbm, forward),
                (stiffness_hbm, stiffness),
                (mass_hbm, mass),
                (conductivity_hbm, conductivity),
                (live_hbm, live),
                (angular_hbm, angular),
            ]
        )
    ]
    for load in loads:
        load.start()

    barrier = pltpu.get_barrier_semaphore()
    row_end = lax.rem(me, 8) == 7
    row_start = lax.rem(me, 8) == 0
    end_pair = row_end & (me < DOM - 1)
    start_pair = row_start & (me > 0)

    def signal(semaphore, freq, dom):
        pl.semaphore_signal(semaphore, inc=1, device_id=(freq, dom), device_id_type=MESH)

    pl.when(end_pair)(lambda: signal(barrier, my_freq, above))
    pl.when(start_pair)(lambda: signal(barrier, my_freq, below))
    for k in NEAR:
        signal(barrier, my_freq, me ^ k)
    for d in (1, 7):
        signal(barrier, lax.rem(my_freq + d, FREQ), me)

    lane = lanes_iota((8, 128))
    sub = rows_iota((8, 128))
    upper = sub < 4

    def halves(ref, n, q):
        first = ref[n, :, pl.ds(pl.multiple_of(128 * q, 128), 128)]
        second = ref[n, :, pl.ds(pl.multiple_of(512 + 128 * q, 128), 128)]
        return jnp.where(upper, spread(first), spread(second))

    loads[0].wait()
    loads[1].wait()
    order_rows = jnp.broadcast_to(order[...], (8, RIM))
    match = jnp.where(rows_iota((RIM, RIM)) == jnp.broadcast_to(order[...], (RIM, RIM)), 1.0, 0.0)
    inverse = lax.dot_general(
        lanes_iota((8, RIM)).astype(F32).astype(BF16),
        match.astype(BF16),
        (((1,), (1,)), ((), ())),
        preferred_element_type=F32,
    ).astype(jnp.int32)
    sources = field_rows(source)

    even = lax.rem(me, 2) == 0
    late_side = lax.rem(me, 2)
    early_side = 1 - late_side
    has_late = (me > 0) & (me < DOM - 1)

    @pl.when(jnp.logical_not(has_late))
    def _():
        for k in range(3):
            rim_in[k, late_side] = jnp.zeros((8, RIM), F32)

    late_peer = jnp.where(even, below, above)

    def rim_copy(k, n):
        side, peer = ((early_side, late_peer), (late_side, me ^ 1))[n]
        return pltpu.make_async_remote_copy(
            src_ref=rim_out.at[k, n, pl.ds(0, 4)],
            dst_ref=rim_in.at[k, side, pl.ds(0, 4)],
            send_sem=rim_send.at[k, n],
            recv_sem=rim_recv.at[k, side],
            device_id=(my_freq, peer),
            device_id_type=MESH,
        )

    def send_late(k, rim):
        rim_out[k, 0] = jnp.where(even, permuted(rim, inverse), rim)
        pl.when(has_late)(rim_copy(k, 0).start)

    def send_early(k, rim):
        rim_out[k, 1] = jnp.where(even, rim, permuted(rim, inverse))
        rim_copy(k, 1).start()

    def late_part(field):
        return jnp.where(even, field[:, :RIM], field[:, EDGES - RIM :])

    def early_part(field):
        return jnp.where(even, field[:, EDGES - RIM :], field[:, :RIM])

    def take_rim(k, side):
        rim = rim_in.at[k, side, pl.ds(0, 4)]
        return pltpu.make_async_copy(rim, rim, rim_recv.at[k, side]).wait

    def received(k, side):
        rim = rim_in[k, side, pl.ds(0, 4)]
        return jnp.concatenate([rim, rim], axis=0)

    def join(field, rim, low_side):
        zero = jnp.zeros((8, RIM), F32)
        return jnp.concatenate(
            [
                field[:, :RIM] + jnp.where(low_side, permuted(rim, order_rows), zero),
                field[:, RIM : EDGES - RIM],
                field[:, EDGES - RIM :] + jnp.where(low_side, zero, rim),
            ],
            axis=1,
        )

    loads[2].wait()

    def tables(q, carry):
        for i in range(6):
            index = halves(edges, i, q)
            ids[q, i] = index
            mapped = pick_rim(order_rows, index)
            in_late = jnp.where(even, index, index - (EDGES - RIM))
            quarter = jnp.where((in_late >= 0) & (in_late < RIM), in_late >> 6, 4)
            for c in range(4):
                hit = jnp.where(quarter == c, 1.0, 0.0)
                late_masks[q, c, :, 128 * i : 128 * (i + 1)] = jnp.concatenate([hit] * PARTS, axis=0).astype(BF16)
            late_ids[q, i] = jnp.where(even, jnp.where(index < RIM, mapped, RIM), jnp.where(index >= EDGES - RIM, index - (EDGES - RIM), RIM))
            wide = index >> 7
            for c in range(CHUNKS):
                hit = jnp.where(wide == c, 1.0, 0.0)
                masks[q, c, :, 128 * i : 128 * (i + 1)] = jnp.concatenate([hit] * PARTS, axis=0).astype(BF16)
        columns = []
        for h in range(2):
            at = pl.ds(pl.multiple_of(512 * h + 128 * q, 128), 128)
            stacked = spread(edges[0, :, at])
            for i in range(1, 6):
                stacked = jnp.where(sub == i, spread(edges[i, :, at]), stacked)
            columns.append(jnp.transpose(stacked & 127))
        across = lanes_iota((128, 128))
        for i in range(6):
            wide = [jnp.broadcast_to(columns[h][:, i : i + 1], (128, 128)) for h in range(2)]
            for h in range(2):
                onehot[q, 128 * i : 128 * (i + 1), 128 * h : 128 * (h + 1)] = jnp.where(
                    wide[h] == across, 1.0, 0.0
                ).astype(BF16)
            short = jnp.where(across < 64, wide[0] & 63, (wide[1] & 63) + 64)
            late_hot[q, 128 * i : 128 * (i + 1)] = jnp.where(short == across, 1.0, 0.0).astype(BF16)
        return carry

    lax.fori_loop(0, AHEAD, tables, 0)

    pl.semaphore_wait(barrier, len(NEAR) + 2 + end_pair.astype(jnp.int32) + start_pair.astype(jnp.int32))
    send_late(0, late_part(sources))
    send_early(0, early_part(sources))
    for k in ONE_HOP:
        signal(round_two, my_freq, me ^ k)
    for d in (1, 7):
        signal(round_two, lax.rem(my_freq + d, FREQ), me)

    lax.fori_loop(AHEAD, GROUPS, tables, 0)

    for n in range(3, 9):
        loads[n].wait()
    omega = jnp.where(sub % 4 < 2, angular[0], angular[1])
    forwards = field_rows(forward)

    def elements(q, carry):
        alive = halves(live, 0, q).astype(F32)
        shift = omega * (halves(conductivity, 0, q) * alive)
        picked = [pick(forwards, ids[q, j]) for j in range(6)]
        for i in range(6):
            running = None
            for j in range(6):
                n = 6 * i + j
                mass_rows = halves(mass, n, q)
                blocks[q, n] = halves(stiffness, n, q) * alive + shift * mass_rows
                product = mass_rows * picked[j]
                running = product if running is None else running + product
            weight[q, i] = omega * running
        return carry

    lax.fori_loop(0, GROUPS, elements, 0)

    pl.semaphore_wait(round_two, len(ONE_HOP) + 2)
    for k in TWO_HOPS:
        signal(round_three, my_freq, me ^ k)
    for d in (2, 6):
        signal(round_three, lax.rem(my_freq + d, FREQ), me)

    def element_values(pick_all, keep=None):
        terms_of = []
        values = []
        for q in range(GROUPS):
            picked = [pick_all(q, i) for i in range(6)]
            if keep is not None:
                for i in range(6):
                    kept[q, i] = picked[i] if keep == 0 else kept[q, i] + picked[i]
            term = weight[q, 0] * picked[0]
            for i in range(1, 6):
                term = term + weight[q, i] * picked[i]
            terms_of.append(term)
            for i in range(6):
                running = blocks[q, 6 * i] * picked[0]
                for j in range(1, 6):
                    running = running + blocks[q, 6 * i + j] * picked[j]
                head = running.astype(BF16).astype(F32)
                values.append(jnp.concatenate([head, running - head], axis=0).astype(BF16))
        return values, jnp.concatenate(terms_of, axis=1)

    def add_up(values, chosen, table, count):
        out = None
        for q in range(GROUPS):
            columns = [
                jnp.concatenate(
                    [values[6 * q + i] * chosen[q, c, :, 128 * i : 128 * (i + 1)] for c in range(count)], axis=0
                )
                for i in range(6)
            ]
            product = lax.dot_general(
                jnp.concatenate(columns, axis=1), table[q], (((1,), (0,)), ((), ())), preferred_element_type=F32
            )
            out = product if out is None else out + product
        return [out[STACK * c : STACK * c + 8] + out[STACK * c + 8 : STACK * c + 16] for c in range(count)]

    def scatter(values):
        pieces = []
        for both in add_up(values, masks, onehot, CHUNKS):
            mixed = jnp.where(upper, both[:, :128], both[:, 128:])
            pieces.append(mixed + pltpu.roll(mixed, 4, 0))
        return jnp.concatenate(pieces, axis=1)

    def scatter_late(values):
        found = add_up(values, late_masks, late_hot, 4)
        turned_lanes = [pltpu.roll(both, 64, 1) for both in found]
        pieces = []
        for c in (0, 2):
            left = jnp.where(upper, found[c], turned_lanes[c])
            right = jnp.where(upper, turned_lanes[c + 1], found[c + 1])
            mixed = jnp.where(lane < 64, left, right)
            pieces.append(mixed + pltpu.roll(mixed, 4, 0))
        return jnp.concatenate(pieces, axis=1)

    def join_early(k, field):
        take_rim(k, early_side)()
        return join(field, received(k, early_side), jnp.logical_not(even))

    def late_rim(k):
        pl.when(has_late)(take_rim(k, late_side))
        return received(k, late_side)

    def apply_early(k, field):
        joined = join_early(k, field)
        values, term = element_values(lambda q, i: pick(joined, ids[q, i]), keep=0 if k == 1 else None)
        return joined, (scatter(values), term)

    def apply_late(k, part):
        rim = late_rim(k)
        values, term = element_values(lambda q, i: pick_rim(rim, late_ids[q, i]), keep=1 if k == 1 else None)
        send_late(k + 1, late_part(part[0]) + scatter_late(values))
        image = part[0] + scatter(values)
        send_early(k + 1, early_part(image))
        return rim, image, part[1] + term

    def pack_sums(start, quantities):
        row = jnp.zeros((8, 128), F32)
        for n, quantity in enumerate(quantities, start):
            column = jnp.sum(quantity, axis=1, keepdims=True)
            row = row + jnp.where((lane == 4 * n + sub) & upper, column, 0.0)
        return jnp.sum(row, axis=0, keepdims=True)

    def send_sums(k, row):
        sums[k, me] = row
        for n in DOM_PEERS:
            pltpu.make_async_remote_copy(
                src_ref=sums.at[k, me],
                dst_ref=sums.at[k, me],
                send_sem=sum_send.at[k],
                recv_sem=sum_recv.at[k],
                device_id=(my_freq, me ^ n),
                device_id_type=MESH,
            ).start()

    def take_sums(k, count):
        rest = sums.at[k, pl.ds(0, DOM - 1)]
        pltpu.make_async_copy(rest, rest, sum_recv.at[k]).wait()
        total = spread(jnp.sum(sums[k], axis=0))
        return [
            jnp.sum(jnp.where(lane == 4 * n + sub % 4, total, 0.0), axis=1, keepdims=True)
            for n in range(count)
        ]

    own = jnp.where(me > 0, 0.0, 1.0).astype(F32)

    base, part = apply_early(0, sources)
    rim, image0, term0 = apply_late(0, part)
    base = join(base, rim, even)
    pl.semaphore_wait(round_three, len(TWO_HOPS) + 2)
    send_sums(0, pack_sums(0, [edge_dot(base, base, own), edge_dot(base, image0)]))
    first, part = apply_early(1, image0)
    rim, image1, term1 = apply_late(1, part)
    first = join(first, rim, even)
    second = join_early(2, image1)
    for q in range(GROUPS):
        for i in range(6):
            kept_next[q, i] = pick(second, ids[q, i])

    norm0, curve0 = take_sums(0, 2)
    alpha0 = norm0 / curve0
    residual = base - alpha0 * first
    residual_image = image0 - alpha0 * image1
    early_sums = pack_sums(
        0,
        [
            edge_dot(residual, residual, own),
            edge_dot(residual, residual_image),
            edge_dot(base, residual_image),
            edge_dot(first, first, own),
            edge_dot(first, image1),
        ],
    )
    near = term0 - alpha0 * term1
    for q in range(GROUPS):
        for i in range(6):
            kept[q, i] = kept[q, i] - alpha0 * kept_next[q, i]

    rim = late_rim(2)
    energy = None
    far = []
    for q in range(GROUPS):
        picked = [kept[q, i] - alpha0 * pick_rim(rim, late_ids[q, i]) for i in range(6)]
        term = weight[q, 0] * picked[0]
        for i in range(1, 6):
            term = term + weight[q, i] * picked[i]
        far.append(term)
        for i in range(6):
            running = 0.5 * (blocks[q, 7 * i] * picked[i])
            for j in range(i + 1, 6):
                running = running + blocks[q, 6 * i + j] * picked[j]
            product = picked[i] * running
            energy = product if energy is None else energy + product
    far = jnp.concatenate(far, axis=1)
    energy = 2.0 * (energy + pltpu.roll(energy, 4, 0))
    turned = first - alpha0 * join(second, rim, even)
    late_sums = pack_sums(
        5,
        [
            edge_dot(turned, turned, own),
            edge_dot(first, turned, own),
            energy,
            edge_dot(image1, turned),
        ],
    )
    send_sums(1, early_sums + late_sums)

    norm1, rr1, br1, bb2, bb3, rr2, br2, rr3, br3 = take_sums(1, 9)
    beta0 = norm1 / norm0
    along1 = rr1 + beta0 * br1
    curve1 = along1 + beta0 * (br1 + beta0 * curve0)
    alpha1 = norm1 / curve1
    square = rr2 + beta0 * (2.0 * br2 + beta0 * bb2)
    norm2 = norm1 - alpha1 * (2.0 * along1 - alpha1 * square)
    self2 = rr1 - alpha1 * (2.0 * (rr2 + beta0 * br2) - alpha1 * (rr3 + beta0 * (2.0 * br3 + beta0 * bb3)))
    cross2 = along1 - alpha1 * square
    beta1 = norm2 / norm1
    curve2 = self2 + beta1 * (2.0 * cross2 + beta1 * curve1)
    alpha2 = norm2 / curve2
    on_d1 = alpha1 + alpha2 * beta1
    total = (
        (alpha0 + on_d1 * beta0) * term0
        + (on_d1 + alpha2) * near
        - (alpha2 * alpha1) * (far + beta0 * term1)
    )

    total = total + pltpu.roll(total, 1, 0)
    total = total + pltpu.roll(total, 2, 0)
    packed = jnp.zeros((8, 128), F32)
    for h in range(2):
        for q in range(GROUPS):
            piece = spread(total[4 * h + 3 : 4 * h + 4, 128 * q : 128 * (q + 1)])
            packed = jnp.where(sub == 4 * h + q, piece, packed)
    terms[my_freq] = packed
    for n in FREQ_PEERS:
        peer = lax.rem(my_freq + n, FREQ)
        pltpu.make_async_remote_copy(
            src_ref=terms.at[my_freq],
            dst_ref=terms.at[my_freq],
            send_sem=term_send,
            recv_sem=term_recv,
            device_id=(peer, me),
            device_id_type=MESH,
        ).start()
    for k in range(3):
        pl.when(has_late)(rim_copy(k, 0).wait_send)
        rim_copy(k, 1).wait_send()
    for k in range(2):
        sent = sums.at[k, pl.ds(0, DOM - 1)]
        pltpu.make_async_copy(sent, sent, sum_send.at[k]).wait()
    rest = terms.at[pl.ds(0, FREQ - 1)]
    pltpu.make_async_copy(rest, rest, term_recv).wait()
    added = terms[0]
    for n in range(1, FREQ):
        added = added + terms[n]
    for r in range(8):
        total_ref[:, 128 * r : 128 * (r + 1)] = added[r : r + 1]
    pltpu.make_async_copy(rest, rest, term_send).wait()


def local(
    angular,
    stiffness,
    mass_matrix,
    conductivity,
    element_edges,
    live_slots,
    adjoint_source,
    forward_field,
    neighbour_map,
):
    hbm = pl.BlockSpec(memory_space=pltpu.MemorySpace.HBM)
    dma = pltpu.SemaphoreType.DMA
    total = pl.pallas_call(
        kernel,
        out_shape=pltpu.VMEM((1, 1024), F32),
        in_specs=[hbm] * 9,
        out_specs=pl.BlockSpec(memory_space=pltpu.MemorySpace.VMEM),
        scratch_shapes=[
            pltpu.SMEM((2,), F32),
            pltpu.VMEM((36, 1, 1024), F32),
            pltpu.VMEM((36, 1, 1024), F32),
            pltpu.VMEM((1, 1, 1024), F32),
            pltpu.VMEM((6, 1, 1024), jnp.int32),
            pltpu.VMEM((1, 1, 1024), jnp.int32),
            pltpu.VMEM((2, 2, 1, EDGES), F32),
            pltpu.VMEM((2, 2, 1, EDGES), F32),
            pltpu.VMEM((1, RIM), jnp.int32),
            pltpu.VMEM((GROUPS, 6, 8, 128), jnp.int32),
            pltpu.VMEM((GROUPS, 6, 8, 128), jnp.int32),
            pltpu.VMEM((GROUPS, CHUNKS, STACK, 768), BF16),
            pltpu.VMEM((GROUPS, 768, 256), BF16),
            pltpu.VMEM((GROUPS, 4, STACK, 768), BF16),
            pltpu.VMEM((GROUPS, 768, 128), BF16),
            pltpu.VMEM((GROUPS, 36, 8, 128), F32),
            pltpu.VMEM((GROUPS, 6, 8, 128), F32),
            pltpu.VMEM((GROUPS, 6, 8, 128), F32),
            pltpu.VMEM((GROUPS, 6, 8, 128), F32),
            pltpu.VMEM((3, 2, 8, RIM), F32),
            pltpu.VMEM((3, 2, 8, RIM), F32),
            pltpu.VMEM((2, DOM, 1, 128), F32),
            pltpu.VMEM((FREQ, 8, 128), F32),
            dma((9,)),
            dma((3, 2)),
            dma((3, 2)),
            dma((3,)),
            dma((3,)),
            dma,
            dma,
            pltpu.SemaphoreType.REGULAR,
            pltpu.SemaphoreType.REGULAR,
        ],
        compiler_params=pltpu.CompilerParams(collective_id=0, has_side_effects=True),
    )(
        angular,
        jnp.transpose(stiffness, (1, 0, 2)),
        jnp.transpose(mass_matrix, (1, 0, 2)),
        conductivity[None],
        jnp.transpose(element_edges, (1, 0, 2)),
        live_slots[None],
        adjoint_source,
        forward_field,
        neighbour_map,
    )
    gradient = -total * live_slots.astype(F32)
    updated = conductivity * jnp.exp(-0.5 * jnp.tanh(gradient))
    return gradient, updated


def solution(mesh):
    return jax.shard_map(
        local,
        mesh=mesh,
        in_specs=(
            P("freq"),
            P("dom", None, None),
            P("dom", None, None),
            P("dom", None),
            P("dom", None, None),
            P("dom", None),
            P("freq", None, "dom", None),
            P("freq", None, "dom", None),
            P("dom", None),
        ),
        out_specs=(P("dom", None), P("dom", None)),
        check_vma=False,
    )
```
